256 devices in a mesh: lev: 4 (over z_hi), gx: 16 (over x, y), gy: 4 (over z_lo, core).
Axes of the slice: x: 4, y: 4, z: 8 (z_hi: 4, z_lo: 2; z = z_hi * 2 + z_lo), core: 2. Of those that a mesh axis runs over, the one named last changes fastest.
Arguments:
- increment: float32 [2, 64, 1024, 512], P(None, 'lev', 'gx', 'gy'), may hold values from -6 to 6
- norm_gain: float32 [2, 64, 1024, 512], P(None, 'lev', 'gx', 'gy'), may hold values from 0.5 to 2
- diffusion_i: float32 [64, 1024, 512], P('lev', 'gx', 'gy'), may hold values from 0.1 to 0.24
- diffusion_j: float32 [64, 1024, 512], P('lev', 'gx', 'gy'), may hold values from 0.1 to 0.24
- sea_mask: int32 [64, 1024, 512], P('lev', 'gx', 'gy'), may hold values from 0 to 1, as said below
- coupling: float32 [128, 128], replicated, may hold values from -0.5 to 0.5
Outputs:
- correlated: float32 [2, 64, 1024, 512], P(None, 'lev', 'gx', 'gy')
The draws below stay inside these ranges and needn't reach their ends.
Inputs may be any that keep to these rules, and one draw needn't show every extreme that they name: `sea_mask`: in every column the sea cells are the levels from the top down to some depth, which may be zero.
All inputs are finite; a program needn't handle non-finite values.
Results may differ from the reference program's by a relative error of at most 0.00009.
Values sent between devices are 32-bit elements; how exact they have to be, the bound alone decides.
A program may use at most 64 MiB of HBM per device.

```python
import math
import jax
import jax.numpy as jnp
from jax import lax

ITERS = 2
NLEV = 64
NI = 1024
NJ = 512


def draw_sea_mask(key, part):
    bottom = jax.random.randint(key, (NI, NJ), 0, NLEV + 1)
    level = lax.broadcasted_iota(jnp.int32, (NLEV, NI, NJ), 0)
    return (level < bottom[None]).astype(jnp.int32)


def levels(stream_key, dims, pieces, least, high):
    def one(position, parts):
        draws = jax.random.uniform(jax.random.fold_in(jax.random.fold_in(stream_key, 6), position), (parts,), jnp.float32, least / len(pieces), high / len(pieces))
        return jnp.repeat(jnp.exp(draws), dims[position] // parts).reshape((-1,) + (1,) * (len(dims) - position - 1))

    loudness = one(*pieces[0])
    for cut in pieces[1:]:
        loudness = loudness * one(*cut)
    return loudness


def bell_draw(stream_key, dims, width, most, cuts=(), kind=jnp.bfloat16):
    level = levels(stream_key, dims, cuts, -0.22, 0.18) if cuts else 1.0
    result = jax.random.normal(stream_key, dims, jnp.float32) * width * level
    return jnp.minimum(jnp.maximum(result, -most), most).astype(kind)


def setup_inputs(seed: int = 0) -> dict:
    splits = jax.random.split(jax.random.key(seed), 7)
    increment = bell_draw(splits[0], (2, NLEV, NI, NJ), 1.0, 6.0, ((1, 4), (2, 16), (3, 4)), jnp.float32)
    norm_gain = jnp.clip(jnp.exp(math.log(2.0) - 1.3862944 * jax.random.uniform(splits[1], (2, NLEV, NI, NJ), jnp.float32) ** levels(splits[1], (2, NLEV, NI, NJ), ((1, 4), (2, 16), (3, 4)), -0.2, 0.2)), 0.5, 2.0)
    diffusion_i = jnp.clip(jnp.exp(math.log(0.24) - 0.8754687 * jax.random.uniform(splits[2], (NLEV, NI, NJ), jnp.float32) ** levels(splits[2], (NLEV, NI, NJ), ((0, 4), (1, 16), (2, 4)), -0.2, 0.2)), 0.1, 0.24)
    diffusion_j = jnp.clip(jnp.exp(math.log(0.24) - 0.8754687 * jax.random.uniform(splits[3], (NLEV, NI, NJ), jnp.float32) ** levels(splits[3], (NLEV, NI, NJ), ((0, 4), (1, 16), (2, 4)), -0.2, 0.2)), 0.1, 0.24)
    sea_mask = draw_sea_mask(jax.random.fold_in(splits[6], 71), 0)
    coupling = bell_draw(splits[5], (2 * NLEV, 2 * NLEV), (2 * NLEV) ** -0.5, 0.5, (), jnp.float32)
    return {"increment": increment, "norm_gain": norm_gain, "diffusion_i": diffusion_i, "diffusion_j": diffusion_j, "sea_mask": sea_mask, "coupling": coupling}


def extend(array, margin):
    array = jnp.concatenate([array[..., -margin:, :], array, array[..., :margin, :]], axis=-2)
    padding = [(0, 0)] * (array.ndim - 1) + [(margin, margin)]
    return jnp.pad(array, padding)


def diffuse(values, coefficients):
    along_i = coefficients[0]
    along_j = coefficients[1]
    ocean = coefficients[2]
    weight_i = along_i[:, :-1, :] * ocean[:, :-1, :] * ocean[:, 1:, :]
    flux_i = weight_i[None] * (values[:, :, 1:, :] - values[:, :, :-1, :])
    weight_j = along_j[:, :, :-1] * ocean[:, :, :-1] * ocean[:, :, 1:]
    flux_j = weight_j[None] * (values[:, :, :, 1:] - values[:, :, :, :-1])
    return (values[:, :, 1:-1, 1:-1] + flux_i[:, :, 1:, 1:-1] - flux_i[:, :, :-1, 1:-1]
            + flux_j[:, :, 1:-1, 1:] - flux_j[:, :, 1:-1, :-1])


def reference(increment, norm_gain, diffusion_i, diffusion_j, sea_mask, coupling):
    ocean = sea_mask.astype(jnp.float32)
    scaled = ocean[None] * norm_gain * increment
    order_count = coupling.shape[0]
    balance = jnp.eye(order_count, dtype=jnp.float32) + coupling
    forward = balance.reshape(2, NLEV, 2, NLEV)
    adjoint_mixed = jnp.einsum('cdab,cdij->abij', forward, scaled, precision=lax.Precision.HIGHEST) * ocean[None]
    coefficients = extend(jnp.stack([diffusion_i, diffusion_j, ocean]), 1)
    spread = adjoint_mixed
    for repeat in range(2 * ITERS):
        spread = diffuse(extend(spread, 1), coefficients)
    forward_mixed = jnp.einsum('abcd,cdij->abij', forward, spread, precision=lax.Precision.HIGHEST)
    return ocean[None] * norm_gain * forward_mixed
```

```python
import jax
import jax.numpy as jnp
from jax import lax
from jax.sharding import PartitionSpec as P

ITERS = 2


def with_halo(x, sides, width, wrap):
    for axis, dim in sides:
        devices, length = (lax.axis_size(axis), x.shape[dim])
        up = [(i, (i + 1) % devices) for i in range(devices if wrap else devices - 1)]
        down = [(j, i) for i, j in up]
        last = lax.slice_in_dim(x, length - width, length, axis=dim)
        first = lax.slice_in_dim(x, 0, width, axis=dim)
        before = lax.ppermute(last, axis, up)
        after = lax.ppermute(first, axis, down)
        x = jnp.concatenate([before, x, after], axis=dim)
    return x


def extend(x, width):
    x = with_halo(x, (("gx", x.ndim - 2),), width, True)
    return with_halo(x, (("gy", x.ndim - 1),), width, False)


def to_columns(x):
    return lax.all_to_all(x, "lev", 2, 1, tiled=True)


def to_levels(x):
    return lax.all_to_all(x, "lev", 1, 2, tiled=True)


def level_mix(fields, matrix):
    columns = to_columns(fields)
    mixed = jnp.einsum("abcd,cdij->abij", matrix, columns, precision=lax.Precision.HIGHEST)
    return to_levels(mixed)


def diffusion(values, weight_i, weight_j, steps):
    for s in range(steps):
        wi = weight_i[:, s:weight_i.shape[1] - s, s:weight_i.shape[2] - s]
        wj = weight_j[:, s:weight_j.shape[1] - s, s:weight_j.shape[2] - s]
        flux_i = wi[None] * (values[:, :, 1:, :] - values[:, :, :-1, :])
        flux_j = wj[None] * (values[:, :, :, 1:] - values[:, :, :, :-1])
        values = (
            values[:, :, 1:-1, 1:-1]
            + flux_i[:, :, 1:, 1:-1]
            - flux_i[:, :, :-1, 1:-1]
            + flux_j[:, :, 1:-1, 1:]
            - flux_j[:, :, 1:-1, :-1]
        )
    return values


def shards(increment, norm_gain, diffusion_i, diffusion_j, sea_mask, coupling):
    steps = 2 * ITERS
    ocean = sea_mask.astype(jnp.float32)
    scaled = ocean[None] * norm_gain * increment
    order_count = coupling.shape[0]
    level_count = order_count // 2
    balance = jnp.eye(order_count, dtype=jnp.float32) + coupling
    forward = balance.reshape(2, level_count, 2, level_count)
    adjoint = jnp.transpose(forward, (2, 3, 0, 1))
    coefs = extend(jnp.stack([diffusion_i, diffusion_j, ocean]), steps)
    along_i, along_j, sea = coefs[0], coefs[1], coefs[2]
    weight_i = along_i[:, :-1, :] * sea[:, :-1, :] * sea[:, 1:, :]
    weight_j = along_j[:, :, :-1] * sea[:, :, :-1] * sea[:, :, 1:]
    adjoint_mixed = level_mix(scaled, adjoint) * ocean[None]
    spread = diffusion(extend(adjoint_mixed, steps), weight_i, weight_j, steps)
    forward_mixed = level_mix(spread, forward)
    return ocean[None] * norm_gain * forward_mixed


def solution(mesh):
    return jax.shard_map(
        shards,
        mesh=mesh,
        in_specs=(
            P(None, "lev", "gx", "gy"),
            P(None, "lev", "gx", "gy"),
            P("lev", "gx", "gy"),
            P("lev", "gx", "gy"),
            P("lev", "gx", "gy"),
            P(),
        ),
        out_specs=P(None, "lev", "gx", "gy"),
        check_vma=False,
    )
```

```python
import jax
import jax.numpy as jnp
from jax import lax
from jax.sharding import PartitionSpec as P

ITERS = 2


def with_halo(x, sides, width, wrap):
    for axis, dim in sides:
        devices, length = (lax.axis_size(axis), x.shape[dim])
        up = [(i, (i + 1) % devices) for i in range(devices if wrap else devices - 1)]
        down = [(j, i) for i, j in up]
        last = lax.slice_in_dim(x, length - width, length, axis=dim)
        first = lax.slice_in_dim(x, 0, width, axis=dim)
        before = lax.ppermute(last, axis, up)
        after = lax.ppermute(first, axis, down)
        x = jnp.concatenate([before, x, after], axis=dim)
    return x


def extend(x, width):
    x = with_halo(x, (("gx", x.ndim - 2),), width, True)
    return with_halo(x, (("gy", x.ndim - 1),), width, False)


def shift(x, step):
    devices = lax.axis_size("lev")
    return lax.ppermute(x, "lev", [(i, (i + step) % devices) for i in range(devices)])


def exchange(blocks):
    half = blocks[2].shape[-1] // 2
    width = blocks[1].shape[-1]
    from_minus = shift(jnp.concatenate([blocks[1], blocks[2][..., :half]], -1), 1)
    from_plus = shift(jnp.concatenate([blocks[3], blocks[2][..., half:]], -1), -1)
    relay_a = shift(from_minus[..., width:], 1)
    relay_b = shift(from_plus[..., width:], -1)
    from_two = jnp.concatenate([relay_a, relay_b], -1)
    return [blocks[0], from_plus[..., :width], from_two, from_minus[..., :width]]


def roll_rows(x, blocks):
    devices = lax.axis_size("lev")
    size = x.shape[2] // devices
    start = blocks * size
    return lax.dynamic_slice_in_dim(jnp.concatenate([x, x], 2), start, x.shape[2], 2)


def to_columns(x):
    devices = lax.axis_size("lev")
    me = lax.axis_index("lev")
    rolled = roll_rows(x, me)
    size = x.shape[2] // devices
    blocks = [rolled[:, :, k * size:(k + 1) * size] for k in range(devices)]
    return jnp.concatenate(exchange(blocks), 1)


def to_levels(y):
    devices = lax.axis_size("lev")
    me = lax.axis_index("lev")
    size = y.shape[1] // devices
    blocks = [y[:, k * size:(k + 1) * size] for k in range(devices)]
    rolled = jnp.concatenate(exchange(blocks), 2)
    return roll_rows(rolled, (devices - me) % devices)


def level_mix(fields, matrix):
    devices = lax.axis_size("lev")
    me = lax.axis_index("lev")
    size = matrix.shape[1] // devices
    rel = jnp.roll(jnp.roll(matrix, -size * me, axis=1), -size * me, axis=3)
    columns = to_columns(fields)
    mixed = jnp.einsum("abcd,cdij->abij", rel, columns, precision=lax.Precision.HIGHEST)
    return to_levels(mixed)


def diffusion(values, weight_i, weight_j, steps):
    for s in range(steps):
        wi = weight_i[:, s:weight_i.shape[1] - s, s:weight_i.shape[2] - s]
        wj = weight_j[:, s:weight_j.shape[1] - s, s:weight_j.shape[2] - s]
        flux_i = wi[None] * (values[:, :, 1:, :] - values[:, :, :-1, :])
        flux_j = wj[None] * (values[:, :, :, 1:] - values[:, :, :, :-1])
        values = (
            values[:, :, 1:-1, 1:-1]
            + flux_i[:, :, 1:, 1:-1]
            - flux_i[:, :, :-1, 1:-1]
            + flux_j[:, :, 1:-1, 1:]
            - flux_j[:, :, 1:-1, :-1]
        )
    return values


def shards(increment, norm_gain, diffusion_i, diffusion_j, sea_mask, coupling):
    steps = 2 * ITERS
    ocean = sea_mask.astype(jnp.float32)
    scaled = ocean[None] * norm_gain * increment
    order_count = coupling.shape[0]
    level_count = order_count // 2
    balance = jnp.eye(order_count, dtype=jnp.float32) + coupling
    forward = balance.reshape(2, level_count, 2, level_count)
    adjoint = jnp.transpose(forward, (2, 3, 0, 1))
    coefs = extend(jnp.stack([diffusion_i, diffusion_j, ocean]), steps)
    along_i, along_j, sea = coefs[0], coefs[1], coefs[2]
    weight_i = along_i[:, :-1, :] * sea[:, :-1, :] * sea[:, 1:, :]
    weight_j = along_j[:, :, :-1] * sea[:, :, :-1] * sea[:, :, 1:]
    adjoint_mixed = level_mix(scaled, adjoint) * ocean[None]
    spread = diffusion(extend(adjoint_mixed, steps), weight_i, weight_j, steps)
    forward_mixed = level_mix(spread, forward)
    return ocean[None] * norm_gain * forward_mixed


def solution(mesh):
    return jax.shard_map(
        shards,
        mesh=mesh,
        in_specs=(
            P(None, "lev", "gx", "gy"),
            P(None, "lev", "gx", "gy"),
            P("lev", "gx", "gy"),
            P("lev", "gx", "gy"),
            P("lev", "gx", "gy"),
            P(),
        ),
        out_specs=P(None, "lev", "gx", "gy"),
        check_vma=False,
    )
```

```python
import jax
import jax.numpy as jnp
from jax import lax
from jax.experimental import pallas as pl
from jax.experimental.pallas import tpu as pltpu
from jax.sharding import PartitionSpec as P

ITERS = 2
MESH = pl.DeviceIdType.MESH


def with_halo(x, sides, width, wrap):
    for axis, dim in sides:
        devices, length = (lax.axis_size(axis), x.shape[dim])
        up = [(i, (i + 1) % devices) for i in range(devices if wrap else devices - 1)]
        down = [(j, i) for i, j in up]
        last = lax.slice_in_dim(x, length - width, length, axis=dim)
        first = lax.slice_in_dim(x, 0, width, axis=dim)
        before = lax.ppermute(last, axis, up)
        after = lax.ppermute(first, axis, down)
        x = jnp.concatenate([before, x, after], axis=dim)
    return x


def extend(x, width):
    x = with_halo(x, (("gx", x.ndim - 2),), width, True)
    return with_halo(x, (("gy", x.ndim - 1),), width, False)


def lev_exchange(x, src_axis, dst_axis, collective):
    n = lax.axis_size("lev")
    out_shape = list(x.shape)
    out_shape[src_axis] //= n
    out_shape[dst_axis] *= n
    src_size = out_shape[src_axis]
    dst_size = x.shape[dst_axis]

    def window(axis, start, size):
        index = [slice(None)] * x.ndim
        index[axis] = pl.ds(start, size)
        return tuple(index)

    def kernel(x_ref, o_ref, send_sem, recv_sem, local_sem):
        me = lax.axis_index("lev")
        gx = lax.axis_index("gx")
        gy = lax.axis_index("gy")
        barrier = pltpu.get_barrier_semaphore()
        for k in range(1, n):
            pl.semaphore_signal(barrier, inc=1, device_id=((me + k) % n, gx, gy), device_id_type=MESH)
        pl.semaphore_wait(barrier, n - 1)
        copies = []
        for k in range(1, n):
            peer = (me + k) % n
            copy = pltpu.make_async_remote_copy(
                src_ref=x_ref.at[window(src_axis, peer * src_size, src_size)],
                dst_ref=o_ref.at[window(dst_axis, me * dst_size, dst_size)],
                send_sem=send_sem.at[k - 1],
                recv_sem=recv_sem.at[k - 1],
                device_id=(peer, gx, gy),
                device_id_type=MESH,
            )
            copy.start()
            copies.append(copy)
        local = pltpu.make_async_copy(
            x_ref.at[window(src_axis, me * src_size, src_size)],
            o_ref.at[window(dst_axis, me * dst_size, dst_size)],
            local_sem,
        )
        local.start()
        local.wait()
        for copy in copies:
            copy.wait()

    return pl.pallas_call(
        kernel,
        out_shape=jax.ShapeDtypeStruct(tuple(out_shape), x.dtype),
        in_specs=[pl.BlockSpec(memory_space=pl.ANY)],
        out_specs=pl.BlockSpec(memory_space=pl.ANY),
        scratch_shapes=[
            pltpu.SemaphoreType.DMA((n - 1,)),
            pltpu.SemaphoreType.DMA((n - 1,)),
            pltpu.SemaphoreType.DMA,
        ],
        compiler_params=pltpu.CompilerParams(collective_id=collective, has_side_effects=True),
    )(x)


def to_columns(x):
    return lev_exchange(x, 2, 1, 0)


def to_levels(x):
    return lev_exchange(x, 1, 2, 1)


def level_mix(fields, matrix):
    columns = to_columns(fields)
    mixed = jnp.einsum("abcd,cdij->abij", matrix, columns, precision=lax.Precision.HIGHEST)
    return to_levels(mixed)


def diffusion(values, weight_i, weight_j, steps):
    for s in range(steps):
        wi = weight_i[:, s:weight_i.shape[1] - s, s:weight_i.shape[2] - s]
        wj = weight_j[:, s:weight_j.shape[1] - s, s:weight_j.shape[2] - s]
        flux_i = wi[None] * (values[:, :, 1:, :] - values[:, :, :-1, :])
        flux_j = wj[None] * (values[:, :, :, 1:] - values[:, :, :, :-1])
        values = (
            values[:, :, 1:-1, 1:-1]
            + flux_i[:, :, 1:, 1:-1]
            - flux_i[:, :, :-1, 1:-1]
            + flux_j[:, :, 1:-1, 1:]
            - flux_j[:, :, 1:-1, :-1]
        )
    return values


def shards(increment, norm_gain, diffusion_i, diffusion_j, sea_mask, coupling):
    steps = 2 * ITERS
    ocean = sea_mask.astype(jnp.float32)
    scaled = ocean[None] * norm_gain * increment
    order_count = coupling.shape[0]
    level_count = order_count // 2
    balance = jnp.eye(order_count, dtype=jnp.float32) + coupling
    forward = balance.reshape(2, level_count, 2, level_count)
    adjoint = jnp.transpose(forward, (2, 3, 0, 1))
    coefs = extend(jnp.stack([diffusion_i, diffusion_j, ocean]), steps)
    along_i, along_j, sea = coefs[0], coefs[1], coefs[2]
    weight_i = along_i[:, :-1, :] * sea[:, :-1, :] * sea[:, 1:, :]
    weight_j = along_j[:, :, :-1] * sea[:, :, :-1] * sea[:, :, 1:]
    adjoint_mixed = level_mix(scaled, adjoint) * ocean[None]
    spread = diffusion(extend(adjoint_mixed, steps), weight_i, weight_j, steps)
    forward_mixed = level_mix(spread, forward)
    return ocean[None] * norm_gain * forward_mixed


def solution(mesh):
    return jax.shard_map(
        shards,
        mesh=mesh,
        in_specs=(
            P(None, "lev", "gx", "gy"),
            P(None, "lev", "gx", "gy"),
            P("lev", "gx", "gy"),
            P("lev", "gx", "gy"),
            P("lev", "gx", "gy"),
            P(),
        ),
        out_specs=P(None, "lev", "gx", "gy"),
        check_vma=False,
    )
```

```python
import jax
import jax.numpy as jnp
from jax import lax
from jax.experimental import pallas as pl
from jax.experimental.pallas import tpu as pltpu
from jax.sharding import PartitionSpec as P

ITERS = 2
MESH = pl.DeviceIdType.MESH


def with_halo(x, sides, width, wrap):
    for axis, dim in sides:
        devices, length = (lax.axis_size(axis), x.shape[dim])
        up = [(i, (i + 1) % devices) for i in range(devices if wrap else devices - 1)]
        down = [(j, i) for i, j in up]
        last = lax.slice_in_dim(x, length - width, length, axis=dim)
        first = lax.slice_in_dim(x, 0, width, axis=dim)
        before = lax.ppermute(last, axis, up)
        after = lax.ppermute(first, axis, down)
        x = jnp.concatenate([before, x, after], axis=dim)
    return x


def extend(x, width):
    x = with_halo(x, (("gx", x.ndim - 2),), width, True)
    return with_halo(x, (("gy", x.ndim - 1),), width, False)


def lev_exchange(x, src_axis, dst_axis, collective):
    n = lax.axis_size("lev")
    out_shape = list(x.shape)
    out_shape[src_axis] //= n
    out_shape[dst_axis] *= n
    src_size = out_shape[src_axis]
    dst_size = x.shape[dst_axis]

    def window(axis, start, size):
        index = [slice(None)] * x.ndim
        index[axis] = pl.ds(start, size)
        return tuple(index)

    def kernel(x_ref, o_ref, send_sem, recv_sem, local_sem):
        me = lax.axis_index("lev")
        gx = lax.axis_index("gx")
        gy = lax.axis_index("gy")
        barrier = pltpu.get_barrier_semaphore()
        for k in range(1, n):
            pl.semaphore_signal(barrier, inc=1, device_id=((me + k) % n, gx, gy), device_id_type=MESH)
        pl.semaphore_wait(barrier, n - 1)
        copies = []
        for k in range(1, n):
            peer = (me + k) % n
            copy = pltpu.make_async_remote_copy(
                src_ref=x_ref.at[window(src_axis, peer * src_size, src_size)],
                dst_ref=o_ref.at[window(dst_axis, me * dst_size, dst_size)],
                send_sem=send_sem.at[k - 1],
                recv_sem=recv_sem.at[k - 1],
                device_id=(peer, gx, gy),
                device_id_type=MESH,
            )
            copy.start()
            copies.append(copy)
        local = pltpu.make_async_copy(
            x_ref.at[window(src_axis, me * src_size, src_size)],
            o_ref.at[window(dst_axis, me * dst_size, dst_size)],
            local_sem,
        )
        local.start()
        local.wait()
        for copy in copies:
            copy.wait()

    return pl.pallas_call(
        kernel,
        out_shape=jax.ShapeDtypeStruct(tuple(out_shape), x.dtype),
        in_specs=[pl.BlockSpec(memory_space=pl.ANY)],
        out_specs=pl.BlockSpec(memory_space=pl.ANY),
        scratch_shapes=[
            pltpu.SemaphoreType.DMA((n - 1,)),
            pltpu.SemaphoreType.DMA((n - 1,)),
            pltpu.SemaphoreType.DMA,
        ],
        compiler_params=pltpu.CompilerParams(collective_id=collective, has_side_effects=True),
    )(x)


def to_columns(x, kernel):
    if kernel:
        return lev_exchange(x, 2, 1, 0)
    return lax.all_to_all(x, "lev", 2, 1, tiled=True)


def to_levels(x, kernel):
    if kernel:
        return lev_exchange(x, 1, 2, 1)
    return lax.all_to_all(x, "lev", 1, 2, tiled=True)


def level_mix(fields, matrix, kernel):
    columns = to_columns(fields, kernel)
    mixed = jnp.einsum("abcd,cdij->abij", matrix, columns, precision=lax.Precision.HIGHEST)
    return to_levels(mixed, kernel)


def diffusion(values, weight_i, weight_j, steps):
    for s in range(steps):
        wi = weight_i[:, s:weight_i.shape[1] - s, s:weight_i.shape[2] - s]
        wj = weight_j[:, s:weight_j.shape[1] - s, s:weight_j.shape[2] - s]
        flux_i = wi[None] * (values[:, :, 1:, :] - values[:, :, :-1, :])
        flux_j = wj[None] * (values[:, :, :, 1:] - values[:, :, :, :-1])
        values = (
            values[:, :, 1:-1, 1:-1]
            + flux_i[:, :, 1:, 1:-1]
            - flux_i[:, :, :-1, 1:-1]
            + flux_j[:, :, 1:-1, 1:]
            - flux_j[:, :, 1:-1, :-1]
        )
    return values


def shards(increment, norm_gain, diffusion_i, diffusion_j, sea_mask, coupling):
    steps = 2 * ITERS
    ocean = sea_mask.astype(jnp.float32)
    scaled = ocean[None] * norm_gain * increment
    order_count = coupling.shape[0]
    level_count = order_count // 2
    balance = jnp.eye(order_count, dtype=jnp.float32) + coupling
    forward = balance.reshape(2, level_count, 2, level_count)
    adjoint = jnp.transpose(forward, (2, 3, 0, 1))
    coefs = extend(jnp.stack([diffusion_i, diffusion_j, ocean]), steps)
    along_i, along_j, sea = coefs[0], coefs[1], coefs[2]
    weight_i = along_i[:, :-1, :] * sea[:, :-1, :] * sea[:, 1:, :]
    weight_j = along_j[:, :, :-1] * sea[:, :, :-1] * sea[:, :, 1:]
    adjoint_mixed = level_mix(scaled, adjoint, False) * ocean[None]
    spread = diffusion(extend(adjoint_mixed, steps), weight_i, weight_j, steps)
    forward_mixed = level_mix(spread, forward, True)
    return ocean[None] * norm_gain * forward_mixed


def solution(mesh):
    return jax.shard_map(
        shards,
        mesh=mesh,
        in_specs=(
            P(None, "lev", "gx", "gy"),
            P(None, "lev", "gx", "gy"),
            P("lev", "gx", "gy"),
            P("lev", "gx", "gy"),
            P("lev", "gx", "gy"),
            P(),
        ),
        out_specs=P(None, "lev", "gx", "gy"),
        check_vma=False,
    )
```

```python
import functools

import jax
import jax.numpy as jnp
from jax import lax
from jax.experimental import pallas as pl
from jax.experimental.pallas import tpu as pltpu
from jax.sharding import PartitionSpec as P

ITERS = 2


def circular(x, width):
    fields, levels, rows, cols = x.shape
    gap_rows = 16 - 2 * width
    up = [(i, (i + 1) % lax.axis_size("gx")) for i in range(lax.axis_size("gx"))]
    down = [(j, i) for i, j in up]
    north = lax.ppermute(x[:, :, rows - width:], "gx", up)
    south = lax.ppermute(x[:, :, :width], "gx", down)
    gap = jnp.zeros((fields, levels, gap_rows, cols), x.dtype)
    tall = jnp.concatenate([x, south, gap, north], 2)
    right = [(i, i + 1) for i in range(lax.axis_size("gy") - 1)]
    left = [(j, i) for i, j in right]
    east = lax.ppermute(tall[..., :width], "gy", left)
    west = lax.ppermute(tall[..., cols - width:], "gy", right)
    middle = jnp.zeros((fields, levels, rows + 16, 128 - 2 * width), x.dtype)
    return jnp.concatenate([tall, east, middle, west], 3)


def diffusion_kernel(steps, rows, cols, v_ref, c_ref, o_ref):
    height, span = v_ref.shape[2], v_ref.shape[3]
    along_i = c_ref[0, 0]
    along_j = c_ref[1, 0]
    sea = c_ref[2, 0]
    weight_i = along_i * sea * pltpu.roll(sea, height - 1, 0)
    weight_j = along_j * sea * pltpu.roll(sea, span - 1, 1)
    for f in range(v_ref.shape[0]):
        values = v_ref[f, 0]
        for s in range(steps):
            flux_i = weight_i * (pltpu.roll(values, height - 1, 0) - values)
            flux_j = weight_j * (pltpu.roll(values, span - 1, 1) - values)
            values = values + flux_i - pltpu.roll(flux_i, 1, 0) + flux_j - pltpu.roll(flux_j, 1, 1)
        o_ref[f, 0] = values[:rows, :cols]


def diffusion(values, coefs, steps):
    fields, levels, rows, cols = values.shape
    ext = circular(values, steps)
    height, span = ext.shape[2], ext.shape[3]
    return pl.pallas_call(
        functools.partial(diffusion_kernel, steps, rows, cols),
        out_shape=jax.ShapeDtypeStruct(values.shape, values.dtype),
        grid=(levels,),
        in_specs=[
            pl.BlockSpec((fields, 1, height, span), lambda l: (0, l, 0, 0)),
            pl.BlockSpec((3, 1, height, span), lambda l: (0, l, 0, 0)),
        ],
        out_specs=pl.BlockSpec((fields, 1, rows, cols), lambda l: (0, l, 0, 0)),
    )(ext, coefs)


def to_columns(x):
    return lax.all_to_all(x, "lev", 2, 1, tiled=True)


def to_levels(x):
    return lax.all_to_all(x, "lev", 1, 2, tiled=True)


def level_mix(fields, matrix):
    columns = to_columns(fields)
    mixed = jnp.einsum("abcd,cdij->abij", matrix, columns, precision=lax.Precision.HIGHEST)
    return to_levels(mixed)


def shards(increment, norm_gain, diffusion_i, diffusion_j, sea_mask, coupling):
    steps = 2 * ITERS
    ocean = sea_mask.astype(jnp.float32)
    scaled = ocean[None] * norm_gain * increment
    order_count = coupling.shape[0]
    level_count = order_count // 2
    balance = jnp.eye(order_count, dtype=jnp.float32) + coupling
    forward = balance.reshape(2, level_count, 2, level_count)
    adjoint = jnp.transpose(forward, (2, 3, 0, 1))
    coefs = circular(jnp.stack([diffusion_i, diffusion_j, ocean]), steps)
    adjoint_mixed = level_mix(scaled, adjoint) * ocean[None]
    spread = diffusion(adjoint_mixed, coefs, steps)
    forward_mixed = level_mix(spread, forward)
    return ocean[None] * norm_gain * forward_mixed


def solution(mesh):
    return jax.shard_map(
        shards,
        mesh=mesh,
        in_specs=(
            P(None, "lev", "gx", "gy"),
            P(None, "lev", "gx", "gy"),
            P("lev", "gx", "gy"),
            P("lev", "gx", "gy"),
            P("lev", "gx", "gy"),
            P(),
        ),
        out_specs=P(None, "lev", "gx", "gy"),
        check_vma=False,
    )
```

```python
import functools

import jax
import jax.numpy as jnp
from jax import lax
from jax.experimental import pallas as pl
from jax.experimental.pallas import tpu as pltpu
from jax.sharding import PartitionSpec as P

ITERS = 2


def neighbour(piece, dx, dy):
    nx = lax.axis_size("gx")
    ny = lax.axis_size("gy")
    pairs = [
        (i * ny + j, ((i + dx) % nx) * ny + j + dy)
        for i in range(nx)
        for j in range(ny)
        if 0 <= j + dy < ny
    ]
    return lax.ppermute(piece, ("gx", "gy"), pairs)


def circular(x, width):
    fields, levels, rows, cols = x.shape
    top, bottom = slice(rows - width, rows), slice(0, width)
    first, last = slice(0, width), slice(cols - width, cols)
    north = neighbour(x[:, :, top], 1, 0)
    south = neighbour(x[:, :, bottom], -1, 0)
    east = neighbour(x[:, :, :, first], 0, -1)
    west = neighbour(x[:, :, :, last], 0, 1)
    north_east = neighbour(x[:, :, top, first], 1, -1)
    south_east = neighbour(x[:, :, bottom, first], -1, -1)
    north_west = neighbour(x[:, :, top, last], 1, 1)
    south_west = neighbour(x[:, :, bottom, last], -1, 1)
    gap = jnp.zeros((fields, levels, 16 - 2 * width, cols), x.dtype)
    tall = jnp.concatenate([x, south, gap, north], 2)
    gap = jnp.zeros((fields, levels, 16 - 2 * width, width), x.dtype)
    east = jnp.concatenate([east, south_east, gap, north_east], 2)
    west = jnp.concatenate([west, south_west, gap, north_west], 2)
    middle = jnp.zeros((fields, levels, rows + 16, 128 - 2 * width), x.dtype)
    return jnp.concatenate([tall, east, middle, west], 3)


def diffusion_kernel(steps, rows, cols, v_ref, c_ref, o_ref):
    height, span = v_ref.shape[2], v_ref.shape[3]
    along_i = c_ref[0, 0]
    along_j = c_ref[1, 0]
    sea = c_ref[2, 0]
    weight_i = along_i * sea * pltpu.roll(sea, height - 1, 0)
    weight_j = along_j * sea * pltpu.roll(sea, span - 1, 1)
    for f in range(v_ref.shape[0]):
        values = v_ref[f, 0]
        for s in range(steps):
            flux_i = weight_i * (pltpu.roll(values, height - 1, 0) - values)
            flux_j = weight_j * (pltpu.roll(values, span - 1, 1) - values)
            values = values + flux_i - pltpu.roll(flux_i, 1, 0) + flux_j - pltpu.roll(flux_j, 1, 1)
        o_ref[f, 0] = values[:rows, :cols]


def diffusion(values, coefs, steps):
    fields, levels, rows, cols = values.shape
    ext = circular(values, steps)
    height, span = ext.shape[2], ext.shape[3]
    return pl.pallas_call(
        functools.partial(diffusion_kernel, steps, rows, cols),
        out_shape=jax.ShapeDtypeStruct(values.shape, values.dtype),
        grid=(levels,),
        in_specs=[
            pl.BlockSpec((fields, 1, height, span), lambda l: (0, l, 0, 0)),
            pl.BlockSpec((3, 1, height, span), lambda l: (0, l, 0, 0)),
        ],
        out_specs=pl.BlockSpec((fields, 1, rows, cols), lambda l: (0, l, 0, 0)),
    )(ext, coefs)


def to_columns(x):
    return lax.all_to_all(x, "lev", 2, 1, tiled=True)


def to_levels(x):
    return lax.all_to_all(x, "lev", 1, 2, tiled=True)


def level_mix(fields, matrix):
    columns = to_columns(fields)
    mixed = jnp.einsum("abcd,cdij->abij", matrix, columns, precision=lax.Precision.HIGHEST)
    return to_levels(mixed)


def shards(increment, norm_gain, diffusion_i, diffusion_j, sea_mask, coupling):
    steps = 2 * ITERS
    ocean = sea_mask.astype(jnp.float32)
    scaled = ocean[None] * norm_gain * increment
    order_count = coupling.shape[0]
    level_count = order_count // 2
    balance = jnp.eye(order_count, dtype=jnp.float32) + coupling
    forward = balance.reshape(2, level_count, 2, level_count)
    adjoint = jnp.transpose(forward, (2, 3, 0, 1))
    coefs = circular(jnp.stack([diffusion_i, diffusion_j, ocean]), steps)
    columns = to_columns(scaled)
    mixed = jnp.einsum("abcd,cdij->abij", adjoint, columns, precision=lax.Precision.HIGHEST)
    coefs, mixed = lax.optimization_barrier((coefs, mixed))
    adjoint_mixed = to_levels(mixed) * ocean[None]
    spread = diffusion(adjoint_mixed, coefs, steps)
    forward_mixed = level_mix(spread, forward)
    return ocean[None] * norm_gain * forward_mixed


def solution(mesh):
    return jax.shard_map(
        shards,
        mesh=mesh,
        in_specs=(
            P(None, "lev", "gx", "gy"),
            P(None, "lev", "gx", "gy"),
            P("lev", "gx", "gy"),
            P("lev", "gx", "gy"),
            P("lev", "gx", "gy"),
            P(),
        ),
        out_specs=P(None, "lev", "gx", "gy"),
        check_vma=False,
    )
```

```python
import functools

import jax
import jax.numpy as jnp
from jax import lax
from jax.experimental import pallas as pl
from jax.experimental.pallas import tpu as pltpu
from jax.sharding import PartitionSpec as P

ITERS = 2


def circular(x, width):
    fields, levels, rows, cols = x.shape
    gap_rows = 16 - 2 * width
    up = [(i, (i + 1) % lax.axis_size("gx")) for i in range(lax.axis_size("gx"))]
    down = [(j, i) for i, j in up]
    north = lax.ppermute(x[:, :, rows - width:], "gx", up)
    south = lax.ppermute(x[:, :, :width], "gx", down)
    gap = jnp.zeros((fields, levels, gap_rows, cols), x.dtype)
    tall = jnp.concatenate([x, south, gap, north], 2)
    right = [(i, i + 1) for i in range(lax.axis_size("gy") - 1)]
    left = [(j, i) for i, j in right]
    east = lax.ppermute(tall[..., :width], "gy", left)
    west = lax.ppermute(tall[..., cols - width:], "gy", right)
    middle = jnp.zeros((fields, levels, rows + 16, 128 - 2 * width), x.dtype)
    return jnp.concatenate([tall, east, middle, west], 3)


def diffusion_kernel(steps, rows, cols, v_ref, o_ref):
    height, span = v_ref.shape[2], v_ref.shape[3]
    fields = o_ref.shape[0]
    along_i = v_ref[fields, 0]
    along_j = v_ref[fields + 1, 0]
    sea = v_ref[fields + 2, 0]
    weight_i = along_i * sea * pltpu.roll(sea, height - 1, 0)
    weight_j = along_j * sea * pltpu.roll(sea, span - 1, 1)
    for f in range(fields):
        values = v_ref[f, 0]
        for s in range(steps):
            flux_i = weight_i * (pltpu.roll(values, height - 1, 0) - values)
            flux_j = weight_j * (pltpu.roll(values, span - 1, 1) - values)
            values = values + flux_i - pltpu.roll(flux_i, 1, 0) + flux_j - pltpu.roll(flux_j, 1, 1)
        o_ref[f, 0] = values[:rows, :cols]


def diffusion(values, coefs, steps):
    fields, levels, rows, cols = values.shape
    ext = circular(jnp.concatenate([values, coefs]), steps)
    height, span = ext.shape[2], ext.shape[3]
    return pl.pallas_call(
        functools.partial(diffusion_kernel, steps, rows, cols),
        out_shape=jax.ShapeDtypeStruct(values.shape, values.dtype),
        grid=(levels,),
        in_specs=[pl.BlockSpec((ext.shape[0], 1, height, span), lambda l: (0, l, 0, 0))],
        out_specs=pl.BlockSpec((fields, 1, rows, cols), lambda l: (0, l, 0, 0)),
    )(ext)


def to_columns(x):
    return lax.all_to_all(x, "lev", 2, 1, tiled=True)


def to_levels(x):
    return lax.all_to_all(x, "lev", 1, 2, tiled=True)


def level_mix(fields, matrix):
    columns = to_columns(fields)
    mixed = jnp.einsum("abcd,cdij->abij", matrix, columns, precision=lax.Precision.HIGHEST)
    return to_levels(mixed)


def shards(increment, norm_gain, diffusion_i, diffusion_j, sea_mask, coupling):
    steps = 2 * ITERS
    ocean = sea_mask.astype(jnp.float32)
    scaled = ocean[None] * norm_gain * increment
    order_count = coupling.shape[0]
    level_count = order_count // 2
    balance = jnp.eye(order_count, dtype=jnp.float32) + coupling
    forward = balance.reshape(2, level_count, 2, level_count)
    adjoint = jnp.transpose(forward, (2, 3, 0, 1))
    coefs = jnp.stack([diffusion_i, diffusion_j, ocean])
    adjoint_mixed = level_mix(scaled, adjoint) * ocean[None]
    spread = diffusion(adjoint_mixed, coefs, steps)
    forward_mixed = level_mix(spread, forward)
    return ocean[None] * norm_gain * forward_mixed


def solution(mesh):
    return jax.shard_map(
        shards,
        mesh=mesh,
        in_specs=(
            P(None, "lev", "gx", "gy"),
            P(None, "lev", "gx", "gy"),
            P("lev", "gx", "gy"),
            P("lev", "gx", "gy"),
            P("lev", "gx", "gy"),
            P(),
        ),
        out_specs=P(None, "lev", "gx", "gy"),
        check_vma=False,
    )
```

```python
import functools

import jax
import jax.numpy as jnp
from jax import lax
from jax.experimental import pallas as pl
from jax.experimental.pallas import tpu as pltpu
from jax.sharding import PartitionSpec as P

ITERS = 2


def circular(x, width):
    fields, levels, rows, cols = x.shape
    gap_rows = 16 - 2 * width
    up = [(i, (i + 1) % lax.axis_size("gx")) for i in range(lax.axis_size("gx"))]
    down = [(j, i) for i, j in up]
    north = lax.ppermute(x[:, :, rows - width:], "gx", up)
    south = lax.ppermute(x[:, :, :width], "gx", down)
    gap = jnp.zeros((fields, levels, gap_rows, cols), x.dtype)
    tall = jnp.concatenate([x, south, gap, north], 2)
    right = [(i, i + 1) for i in range(lax.axis_size("gy") - 1)]
    left = [(j, i) for i, j in right]
    east = lax.ppermute(tall[..., :width], "gy", left)
    west = lax.ppermute(tall[..., cols - width:], "gy", right)
    middle = jnp.zeros((fields, levels, rows + 16, 128 - 2 * width), x.dtype)
    return jnp.concatenate([tall, east, middle, west], 3)


def diffusion_kernel(steps, rows, cols, v_ref, o_ref):
    height, span = v_ref.shape[2], v_ref.shape[3]
    fields = o_ref.shape[0]
    along_i = v_ref[fields, 0]
    along_j = v_ref[fields + 1, 0]
    sea = v_ref[fields + 2, 0]
    weight_i = along_i * sea * pltpu.roll(sea, height - 1, 0)
    weight_j = along_j * sea * pltpu.roll(sea, span - 1, 1)
    for f in range(fields):
        values = v_ref[f, 0]
        for s in range(steps):
            flux_i = weight_i * (pltpu.roll(values, height - 1, 0) - values)
            flux_j = weight_j * (pltpu.roll(values, span - 1, 1) - values)
            values = values + flux_i - pltpu.roll(flux_i, 1, 0) + flux_j - pltpu.roll(flux_j, 1, 1)
        o_ref[f, 0] = values[:rows, :cols]


def diffusion(values, coefs, steps):
    fields, levels, rows, cols = values.shape
    ext = jnp.concatenate([circular(values, steps), coefs])
    height, span = ext.shape[2], ext.shape[3]
    return pl.pallas_call(
        functools.partial(diffusion_kernel, steps, rows, cols),
        out_shape=jax.ShapeDtypeStruct(values.shape, values.dtype),
        grid=(levels,),
        in_specs=[pl.BlockSpec((ext.shape[0], 1, height, span), lambda l: (0, l, 0, 0))],
        out_specs=pl.BlockSpec((fields, 1, rows, cols), lambda l: (0, l, 0, 0)),
    )(ext)


def to_columns(x):
    return lax.all_to_all(x, "lev", 2, 1, tiled=True)


def to_levels(x):
    return lax.all_to_all(x, "lev", 1, 2, tiled=True)


def level_mix(fields, matrix):
    columns = to_columns(fields)
    mixed = jnp.einsum("abcd,cdij->abij", matrix, columns, precision=lax.Precision.HIGHEST)
    return to_levels(mixed)


def shards(increment, norm_gain, diffusion_i, diffusion_j, sea_mask, coupling):
    steps = 2 * ITERS
    ocean = sea_mask.astype(jnp.float32)
    scaled = ocean[None] * norm_gain * increment
    order_count = coupling.shape[0]
    level_count = order_count // 2
    balance = jnp.eye(order_count, dtype=jnp.float32) + coupling
    forward = balance.reshape(2, level_count, 2, level_count)
    adjoint = jnp.transpose(forward, (2, 3, 0, 1))
    coefs = circular(jnp.stack([diffusion_i, diffusion_j, ocean]), steps)
    columns = to_columns(scaled)
    mixed = jnp.einsum("abcd,cdij->abij", adjoint, columns, precision=lax.Precision.HIGHEST)
    coefs, mixed = lax.optimization_barrier((coefs, mixed))
    adjoint_mixed = to_levels(mixed) * ocean[None]
    spread = diffusion(adjoint_mixed, coefs, steps)
    forward_mixed = level_mix(spread, forward)
    return ocean[None] * norm_gain * forward_mixed


def solution(mesh):
    return jax.shard_map(
        shards,
        mesh=mesh,
        in_specs=(
            P(None, "lev", "gx", "gy"),
            P(None, "lev", "gx", "gy"),
            P("lev", "gx", "gy"),
            P("lev", "gx", "gy"),
            P("lev", "gx", "gy"),
            P(),
        ),
        out_specs=P(None, "lev", "gx", "gy"),
        check_vma=False,
    )
```

```python
import functools

import jax
import jax.numpy as jnp
from jax import lax
from jax.experimental import pallas as pl
from jax.experimental.pallas import tpu as pltpu
from jax.sharding import PartitionSpec as P

ITERS = 2
MESH = pl.DeviceIdType.MESH


def circular(x, width):
    fields, levels, rows, cols = x.shape
    gap_rows = 16 - 2 * width
    up = [(i, (i + 1) % lax.axis_size("gx")) for i in range(lax.axis_size("gx"))]
    down = [(j, i) for i, j in up]
    north = lax.ppermute(x[:, :, rows - width:], "gx", up)
    south = lax.ppermute(x[:, :, :width], "gx", down)
    gap = jnp.zeros((fields, levels, gap_rows, cols), x.dtype)
    tall = jnp.concatenate([x, south, gap, north], 2)
    right = [(i, i + 1) for i in range(lax.axis_size("gy") - 1)]
    left = [(j, i) for i, j in right]
    east = lax.ppermute(tall[..., :width], "gy", left)
    west = lax.ppermute(tall[..., cols - width:], "gy", right)
    middle = jnp.zeros((fields, levels, rows + 16, 128 - 2 * width), x.dtype)
    return jnp.concatenate([tall, east, middle, west], 3)


def diffusion_kernel(steps, rows, cols, v_ref, o_ref):
    height, span = v_ref.shape[2], v_ref.shape[3]
    fields = o_ref.shape[0]
    along_i = v_ref[fields, 0]
    along_j = v_ref[fields + 1, 0]
    sea = v_ref[fields + 2, 0]
    weight_i = along_i * sea * pltpu.roll(sea, height - 1, 0)
    weight_j = along_j * sea * pltpu.roll(sea, span - 1, 1)
    for f in range(fields):
        values = v_ref[f, 0]
        for s in range(steps):
            flux_i = weight_i * (pltpu.roll(values, height - 1, 0) - values)
            flux_j = weight_j * (pltpu.roll(values, span - 1, 1) - values)
            values = values + flux_i - pltpu.roll(flux_i, 1, 0) + flux_j - pltpu.roll(flux_j, 1, 1)
        o_ref[f, 0] = values[:rows, :cols]


def diffusion(values, coefs, steps):
    fields, levels, rows, cols = values.shape
    ext = jnp.concatenate([circular(values, steps), coefs])
    height, span = ext.shape[2], ext.shape[3]
    return pl.pallas_call(
        functools.partial(diffusion_kernel, steps, rows, cols),
        out_shape=jax.ShapeDtypeStruct(values.shape, values.dtype),
        grid=(levels,),
        in_specs=[pl.BlockSpec((ext.shape[0], 1, height, span), lambda l: (0, l, 0, 0))],
        out_specs=pl.BlockSpec((fields, 1, rows, cols), lambda l: (0, l, 0, 0)),
    )(ext)


def lev_exchange(x, src_axis, dst_axis, half_axis, collective):
    n = lax.axis_size("lev")
    assert half_axis == src_axis
    out_shape = list(x.shape)
    out_shape[src_axis] //= n
    out_shape[dst_axis] *= n
    src_size = out_shape[src_axis]
    dst_size = x.shape[dst_axis]
    half = src_size // 2
    relay_shape = list(out_shape)
    relay_shape[dst_axis] = dst_size
    relay_shape[half_axis] = half

    def window(axis, start, size, h=None):
        index = [slice(None)] * x.ndim
        index[axis] = pl.ds(start, size)
        if h is not None:
            if half_axis == axis:
                index[axis] = pl.ds(start + h * half, half)
            else:
                index[half_axis] = pl.ds(h * half, half)
        return tuple(index)

    def kernel(x_ref, o_ref, relay, send_sem, recv_sem, local_sem):
        me = lax.axis_index("lev")
        gx = lax.axis_index("gx")
        gy = lax.axis_index("gy")
        right = (me + 1) % n
        left = (me + n - 1) % n
        opposite = (me + 2) % n
        barrier = pltpu.get_barrier_semaphore()
        for peer in (left, right):
            pl.semaphore_signal(barrier, inc=1, device_id=(peer, gx, gy), device_id_type=MESH)
        pl.semaphore_wait(barrier, 2)

        def remote(src, dst, slot, peer):
            return pltpu.make_async_remote_copy(
                src_ref=src, dst_ref=dst, send_sem=send_sem.at[slot], recv_sem=recv_sem.at[slot],
                device_id=(peer, gx, gy), device_id_type=MESH,
            )

        to_right = remote(x_ref.at[window(src_axis, right * src_size, src_size)],
                          o_ref.at[window(dst_axis, me * dst_size, dst_size)], 0, right)
        to_left = remote(x_ref.at[window(src_axis, left * src_size, src_size)],
                         o_ref.at[window(dst_axis, me * dst_size, dst_size)], 1, left)
        via_right = remote(x_ref.at[window(src_axis, opposite * src_size, src_size, 0)], relay.at[0], 2, right)
        via_left = remote(x_ref.at[window(src_axis, opposite * src_size, src_size, 1)], relay.at[1], 3, left)
        for copy in (via_right, via_left, to_right, to_left):
            copy.start()
        local = pltpu.make_async_copy(
            x_ref.at[window(src_axis, me * src_size, src_size)],
            o_ref.at[window(dst_axis, me * dst_size, dst_size)],
            local_sem,
        )
        local.start()
        via_right.wait_recv()
        on_right = remote(relay.at[0], o_ref.at[window(dst_axis, left * dst_size, dst_size, 0)], 4, right)
        on_right.start()
        via_left.wait_recv()
        on_left = remote(relay.at[1], o_ref.at[window(dst_axis, right * dst_size, dst_size, 1)], 5, left)
        on_left.start()
        local.wait()
        via_right.wait_send()
        via_left.wait_send()
        for copy in (to_right, to_left, on_right, on_left):
            copy.wait()

    return pl.pallas_call(
        kernel,
        out_shape=jax.ShapeDtypeStruct(tuple(out_shape), x.dtype),
        in_specs=[pl.BlockSpec(memory_space=pl.ANY)],
        out_specs=pl.BlockSpec(memory_space=pl.ANY),
        scratch_shapes=[
            pltpu.VMEM((2,) + tuple(relay_shape), x.dtype),
            pltpu.SemaphoreType.DMA((6,)),
            pltpu.SemaphoreType.DMA((6,)),
            pltpu.SemaphoreType.DMA,
        ],
        compiler_params=pltpu.CompilerParams(collective_id=collective, has_side_effects=True),
    )(x)


def to_columns(x, kernel=True):
    if kernel:
        return lev_exchange(x, 2, 1, 2, 0)
    return lax.all_to_all(x, "lev", 2, 1, tiled=True)


def to_levels(x, kernel=True):
    if kernel:
        return lev_exchange(x, 1, 2, 1, 1)
    return lax.all_to_all(x, "lev", 1, 2, tiled=True)


def level_mix(fields, matrix):
    columns = to_columns(fields)
    mixed = jnp.einsum("abcd,cdij->abij", matrix, columns, precision=lax.Precision.HIGHEST)
    return to_levels(mixed)


def shards(increment, norm_gain, diffusion_i, diffusion_j, sea_mask, coupling):
    steps = 2 * ITERS
    ocean = sea_mask.astype(jnp.float32)
    scaled = ocean[None] * norm_gain * increment
    order_count = coupling.shape[0]
    level_count = order_count // 2
    balance = jnp.eye(order_count, dtype=jnp.float32) + coupling
    forward = balance.reshape(2, level_count, 2, level_count)
    adjoint = jnp.transpose(forward, (2, 3, 0, 1))
    coefs = circular(jnp.stack([diffusion_i, diffusion_j, ocean]), steps)
    columns = to_columns(scaled, False)
    mixed = jnp.einsum("abcd,cdij->abij", adjoint, columns, precision=lax.Precision.HIGHEST)
    coefs, mixed = lax.optimization_barrier((coefs, mixed))
    adjoint_mixed = to_levels(mixed) * ocean[None]
    spread = diffusion(adjoint_mixed, coefs, steps)
    forward_mixed = level_mix(spread, forward)
    return ocean[None] * norm_gain * forward_mixed


def solution(mesh):
    return jax.shard_map(
        shards,
        mesh=mesh,
        in_specs=(
            P(None, "lev", "gx", "gy"),
            P(None, "lev", "gx", "gy"),
            P("lev", "gx", "gy"),
            P("lev", "gx", "gy"),
            P("lev", "gx", "gy"),
            P(),
        ),
        out_specs=P(None, "lev", "gx", "gy"),
        check_vma=False,
    )
```

```python
import functools

import jax
import jax.numpy as jnp
from jax import lax
from jax.experimental import pallas as pl
from jax.experimental.pallas import tpu as pltpu
from jax.sharding import PartitionSpec as P

ITERS = 2
MESH = pl.DeviceIdType.MESH


def circular(x, width):
    fields, levels, rows, cols = x.shape
    gap_rows = 16 - 2 * width
    up = [(i, (i + 1) % lax.axis_size("gx")) for i in range(lax.axis_size("gx"))]
    down = [(j, i) for i, j in up]
    north = lax.ppermute(x[:, :, rows - width:], "gx", up)
    south = lax.ppermute(x[:, :, :width], "gx", down)
    gap = jnp.zeros((fields, levels, gap_rows, cols), x.dtype)
    tall = jnp.concatenate([x, south, gap, north], 2)
    right = [(i, i + 1) for i in range(lax.axis_size("gy") - 1)]
    left = [(j, i) for i, j in right]
    east = lax.ppermute(tall[..., :width], "gy", left)
    west = lax.ppermute(tall[..., cols - width:], "gy", right)
    middle = jnp.zeros((fields, levels, rows + 16, 128 - 2 * width), x.dtype)
    return jnp.concatenate([tall, east, middle, west], 3)


def diffusion_kernel(steps, rows, cols, v_ref, o_ref):
    fields, depth = o_ref.shape[0], o_ref.shape[1]
    height, span = v_ref.shape[2], v_ref.shape[3]
    for level in range(depth):
        along_i = v_ref[fields, level]
        along_j = v_ref[fields + 1, level]
        sea = v_ref[fields + 2, level]
        weight_i = along_i * sea * pltpu.roll(sea, height - 1, 0)
        weight_j = along_j * sea * pltpu.roll(sea, span - 1, 1)
        for f in range(fields):
            values = v_ref[f, level]
            for s in range(steps):
                flux_i = weight_i * (pltpu.roll(values, height - 1, 0) - values)
                flux_j = weight_j * (pltpu.roll(values, span - 1, 1) - values)
                values = values + flux_i - pltpu.roll(flux_i, 1, 0) + flux_j - pltpu.roll(flux_j, 1, 1)
            o_ref[f, level] = values[:rows, :cols]


def diffusion(values, coefs, steps):
    fields, levels, rows, cols = values.shape
    ext = jnp.concatenate([circular(values, steps), coefs])
    height, span = ext.shape[2], ext.shape[3]
    return pl.pallas_call(
        functools.partial(diffusion_kernel, steps, rows, cols),
        out_shape=jax.ShapeDtypeStruct(values.shape, values.dtype),
        grid=(levels // 4,),
        in_specs=[pl.BlockSpec((ext.shape[0], 4, height, span), lambda l: (0, l, 0, 0))],
        out_specs=pl.BlockSpec((fields, 4, rows, cols), lambda l: (0, l, 0, 0)),
    )(ext)


def lev_exchange(x, src_axis, dst_axis, half_axis, collective):
    n = lax.axis_size("lev")
    assert half_axis == src_axis
    out_shape = list(x.shape)
    out_shape[src_axis] //= n
    out_shape[dst_axis] *= n
    src_size = out_shape[src_axis]
    dst_size = x.shape[dst_axis]
    half = src_size // 2
    relay_shape = list(out_shape)
    relay_shape[dst_axis] = dst_size
    relay_shape[half_axis] = half

    def window(axis, start, size, h=None):
        index = [slice(None)] * x.ndim
        index[axis] = pl.ds(start, size)
        if h is not None:
            if half_axis == axis:
                index[axis] = pl.ds(start + h * half, half)
            else:
                index[half_axis] = pl.ds(h * half, half)
        return tuple(index)

    def kernel(x_ref, o_ref, relay, send_sem, recv_sem, local_sem):
        me = lax.axis_index("lev")
        gx = lax.axis_index("gx")
        gy = lax.axis_index("gy")
        right = (me + 1) % n
        left = (me + n - 1) % n
        opposite = (me + 2) % n
        barrier = pltpu.get_barrier_semaphore()
        for peer in (left, right):
            pl.semaphore_signal(barrier, inc=1, device_id=(peer, gx, gy), device_id_type=MESH)
        pl.semaphore_wait(barrier, 2)

        def remote(src, dst, slot, peer):
            return pltpu.make_async_remote_copy(
                src_ref=src, dst_ref=dst, send_sem=send_sem.at[slot], recv_sem=recv_sem.at[slot],
                device_id=(peer, gx, gy), device_id_type=MESH,
            )

        to_right = remote(x_ref.at[window(src_axis, right * src_size, src_size)],
                          o_ref.at[window(dst_axis, me * dst_size, dst_size)], 0, right)
        to_left = remote(x_ref.at[window(src_axis, left * src_size, src_size)],
                         o_ref.at[window(dst_axis, me * dst_size, dst_size)], 1, left)
        via_right = remote(x_ref.at[window(src_axis, opposite * src_size, src_size, 0)], relay.at[0], 2, right)
        via_left = remote(x_ref.at[window(src_axis, opposite * src_size, src_size, 1)], relay.at[1], 3, left)
        for copy in (via_right, via_left, to_right, to_left):
            copy.start()
        local = pltpu.make_async_copy(
            x_ref.at[window(src_axis, me * src_size, src_size)],
            o_ref.at[window(dst_axis, me * dst_size, dst_size)],
            local_sem,
        )
        local.start()
        via_right.wait_recv()
        on_right = remote(relay.at[0], o_ref.at[window(dst_axis, left * dst_size, dst_size, 0)], 4, right)
        on_right.start()
        via_left.wait_recv()
        on_left = remote(relay.at[1], o_ref.at[window(dst_axis, right * dst_size, dst_size, 1)], 5, left)
        on_left.start()
        local.wait()
        via_right.wait_send()
        via_left.wait_send()
        for copy in (to_right, to_left, on_right, on_left):
            copy.wait()

    return pl.pallas_call(
        kernel,
        out_shape=jax.ShapeDtypeStruct(tuple(out_shape), x.dtype),
        in_specs=[pl.BlockSpec(memory_space=pl.ANY)],
        out_specs=pl.BlockSpec(memory_space=pl.ANY),
        scratch_shapes=[
            pltpu.VMEM((2,) + tuple(relay_shape), x.dtype),
            pltpu.SemaphoreType.DMA((6,)),
            pltpu.SemaphoreType.DMA((6,)),
            pltpu.SemaphoreType.DMA,
        ],
        compiler_params=pltpu.CompilerParams(collective_id=collective, has_side_effects=True),
    )(x)


def to_columns(x, kernel=True):
    if kernel:
        return lev_exchange(x, 2, 1, 2, 0)
    return lax.all_to_all(x, "lev", 2, 1, tiled=True)


def to_levels(x, kernel=True):
    if kernel:
        return lev_exchange(x, 1, 2, 1, 1)
    return lax.all_to_all(x, "lev", 1, 2, tiled=True)


def level_mix(fields, matrix):
    columns = to_columns(fields)
    mixed = jnp.einsum("abcd,cdij->abij", matrix, columns, precision=lax.Precision.HIGHEST)
    return to_levels(mixed)


def shards(increment, norm_gain, diffusion_i, diffusion_j, sea_mask, coupling):
    steps = 2 * ITERS
    ocean = sea_mask.astype(jnp.float32)
    scaled = ocean[None] * norm_gain * increment
    order_count = coupling.shape[0]
    level_count = order_count // 2
    balance = jnp.eye(order_count, dtype=jnp.float32) + coupling
    forward = balance.reshape(2, level_count, 2, level_count)
    adjoint = jnp.transpose(forward, (2, 3, 0, 1))
    coefs = circular(jnp.stack([diffusion_i, diffusion_j, ocean]), steps)
    columns = to_columns(scaled, False)
    mixed = jnp.einsum("abcd,cdij->abij", adjoint, columns, precision=lax.Precision.HIGHEST)
    coefs, mixed = lax.optimization_barrier((coefs, mixed))
    adjoint_mixed = to_levels(mixed) * ocean[None]
    spread = diffusion(adjoint_mixed, coefs, steps)
    forward_mixed = level_mix(spread, forward)
    return ocean[None] * norm_gain * forward_mixed


def solution(mesh):
    return jax.shard_map(
        shards,
        mesh=mesh,
        in_specs=(
            P(None, "lev", "gx", "gy"),
            P(None, "lev", "gx", "gy"),
            P("lev", "gx", "gy"),
            P("lev", "gx", "gy"),
            P("lev", "gx", "gy"),
            P(),
        ),
        out_specs=P(None, "lev", "gx", "gy"),
        check_vma=False,
    )
```

```python
import functools

import jax
import jax.numpy as jnp
from jax import lax
from jax.experimental import pallas as pl
from jax.experimental.pallas import tpu as pltpu
from jax.sharding import PartitionSpec as P

ITERS = 2
MESH = pl.DeviceIdType.MESH


def circular(x, width):
    fields, levels, rows, cols = x.shape
    gap_rows = 16 - 2 * width
    up = [(i, (i + 1) % lax.axis_size("gx")) for i in range(lax.axis_size("gx"))]
    down = [(j, i) for i, j in up]
    north = lax.ppermute(x[:, :, rows - width:], "gx", up)
    south = lax.ppermute(x[:, :, :width], "gx", down)
    gap = jnp.zeros((fields, levels, gap_rows, cols), x.dtype)
    tall = jnp.concatenate([x, south, gap, north], 2)
    right = [(i, i + 1) for i in range(lax.axis_size("gy") - 1)]
    left = [(j, i) for i, j in right]
    east = lax.ppermute(tall[..., :width], "gy", left)
    west = lax.ppermute(tall[..., cols - width:], "gy", right)
    middle = jnp.zeros((fields, levels, rows + 16, 128 - 2 * width), x.dtype)
    return jnp.concatenate([tall, east, middle, west], 3)


def diffusion_kernel(steps, rows, cols, v_ref, o_ref):
    height, span = v_ref.shape[2], v_ref.shape[3]
    fields = o_ref.shape[0]
    along_i = v_ref[fields, 0]
    along_j = v_ref[fields + 1, 0]
    sea = v_ref[fields + 2, 0]
    weight_i = along_i * sea * pltpu.roll(sea, height - 1, 0)
    weight_j = along_j * sea * pltpu.roll(sea, span - 1, 1)
    for f in range(fields):
        values = v_ref[f, 0]
        for s in range(steps):
            flux_i = weight_i * (pltpu.roll(values, height - 1, 0) - values)
            flux_j = weight_j * (pltpu.roll(values, span - 1, 1) - values)
            values = values + flux_i - pltpu.roll(flux_i, 1, 0) + flux_j - pltpu.roll(flux_j, 1, 1)
        o_ref[f, 0] = values[:rows, :cols]


def diffusion(values, coefs, steps):
    fields, levels, rows, cols = values.shape
    ext = circular(jnp.concatenate([values, coefs]), steps)
    height, span = ext.shape[2], ext.shape[3]
    return pl.pallas_call(
        functools.partial(diffusion_kernel, steps, rows, cols),
        out_shape=jax.ShapeDtypeStruct(values.shape, values.dtype),
        grid=(levels,),
        in_specs=[pl.BlockSpec((ext.shape[0], 1, height, span), lambda l: (0, l, 0, 0))],
        out_specs=pl.BlockSpec((fields, 1, rows, cols), lambda l: (0, l, 0, 0)),
    )(ext)


def lev_exchange(x, src_axis, dst_axis, half_axis, collective):
    n = lax.axis_size("lev")
    assert half_axis == src_axis
    out_shape = list(x.shape)
    out_shape[src_axis] //= n
    out_shape[dst_axis] *= n
    src_size = out_shape[src_axis]
    dst_size = x.shape[dst_axis]
    half = src_size // 2
    relay_shape = list(out_shape)
    relay_shape[dst_axis] = dst_size
    relay_shape[half_axis] = half

    def window(axis, start, size, h=None):
        index = [slice(None)] * x.ndim
        index[axis] = pl.ds(start, size)
        if h is not None:
            if half_axis == axis:
                index[axis] = pl.ds(start + h * half, half)
            else:
                index[half_axis] = pl.ds(h * half, half)
        return tuple(index)

    def kernel(x_ref, o_ref, relay, send_sem, recv_sem, local_sem):
        me = lax.axis_index("lev")
        gx = lax.axis_index("gx")
        gy = lax.axis_index("gy")
        right = (me + 1) % n
        left = (me + n - 1) % n
        opposite = (me + 2) % n
        barrier = pltpu.get_barrier_semaphore()
        for peer in (left, right):
            pl.semaphore_signal(barrier, inc=1, device_id=(peer, gx, gy), device_id_type=MESH)
        pl.semaphore_wait(barrier, 2)

        def remote(src, dst, slot, peer):
            return pltpu.make_async_remote_copy(
                src_ref=src, dst_ref=dst, send_sem=send_sem.at[slot], recv_sem=recv_sem.at[slot],
                device_id=(peer, gx, gy), device_id_type=MESH,
            )

        to_right = remote(x_ref.at[window(src_axis, right * src_size, src_size)],
                          o_ref.at[window(dst_axis, me * dst_size, dst_size)], 0, right)
        to_left = remote(x_ref.at[window(src_axis, left * src_size, src_size)],
                         o_ref.at[window(dst_axis, me * dst_size, dst_size)], 1, left)
        via_right = remote(x_ref.at[window(src_axis, opposite * src_size, src_size, 0)], relay.at[0], 2, right)
        via_left = remote(x_ref.at[window(src_axis, opposite * src_size, src_size, 1)], relay.at[1], 3, left)
        for copy in (via_right, via_left, to_right, to_left):
            copy.start()
        local = pltpu.make_async_copy(
            x_ref.at[window(src_axis, me * src_size, src_size)],
            o_ref.at[window(dst_axis, me * dst_size, dst_size)],
            local_sem,
        )
        local.start()
        via_right.wait_recv()
        on_right = remote(relay.at[0], o_ref.at[window(dst_axis, left * dst_size, dst_size, 0)], 4, right)
        on_right.start()
        via_left.wait_recv()
        on_left = remote(relay.at[1], o_ref.at[window(dst_axis, right * dst_size, dst_size, 1)], 5, left)
        on_left.start()
        local.wait()
        via_right.wait_send()
        via_left.wait_send()
        for copy in (to_right, to_left, on_right, on_left):
            copy.wait()

    return pl.pallas_call(
        kernel,
        out_shape=jax.ShapeDtypeStruct(tuple(out_shape), x.dtype),
        in_specs=[pl.BlockSpec(memory_space=pl.ANY)],
        out_specs=pl.BlockSpec(memory_space=pl.ANY),
        scratch_shapes=[
            pltpu.VMEM((2,) + tuple(relay_shape), x.dtype),
            pltpu.SemaphoreType.DMA((6,)),
            pltpu.SemaphoreType.DMA((6,)),
            pltpu.SemaphoreType.DMA,
        ],
        compiler_params=pltpu.CompilerParams(collective_id=collective, has_side_effects=True),
    )(x)


def to_columns(x, kernel=True):
    if kernel:
        return lev_exchange(x, 2, 1, 2, 0)
    return lax.all_to_all(x, "lev", 2, 1, tiled=True)


def to_levels(x, kernel=True):
    if kernel:
        return lev_exchange(x, 1, 2, 1, 1)
    return lax.all_to_all(x, "lev", 1, 2, tiled=True)


def level_mix(fields, matrix):
    columns = to_columns(fields)
    mixed = jnp.einsum("abcd,cdij->abij", matrix, columns, precision=lax.Precision.HIGHEST)
    return to_levels(mixed)


def shards(increment, norm_gain, diffusion_i, diffusion_j, sea_mask, coupling):
    steps = 2 * ITERS
    ocean = sea_mask.astype(jnp.float32)
    scaled = ocean[None] * norm_gain * increment
    order_count = coupling.shape[0]
    level_count = order_count // 2
    balance = jnp.eye(order_count, dtype=jnp.float32) + coupling
    forward = balance.reshape(2, level_count, 2, level_count)
    adjoint = jnp.transpose(forward, (2, 3, 0, 1))
    coefs = jnp.stack([diffusion_i, diffusion_j, ocean])
    adjoint_mixed = level_mix(scaled, adjoint) * ocean[None]
    spread = diffusion(adjoint_mixed, coefs, steps)
    forward_mixed = level_mix(spread, forward)
    return ocean[None] * norm_gain * forward_mixed


def solution(mesh):
    return jax.shard_map(
        shards,
        mesh=mesh,
        in_specs=(
            P(None, "lev", "gx", "gy"),
            P(None, "lev", "gx", "gy"),
            P("lev", "gx", "gy"),
            P("lev", "gx", "gy"),
            P("lev", "gx", "gy"),
            P(),
        ),
        out_specs=P(None, "lev", "gx", "gy"),
        check_vma=False,
    )
```

```python
import functools

import jax
import jax.numpy as jnp
from jax import lax
from jax.experimental import pallas as pl
from jax.experimental.pallas import tpu as pltpu
from jax.sharding import PartitionSpec as P

ITERS = 2
MESH = pl.DeviceIdType.MESH


def circular(x, width):
    fields, levels, rows, cols = x.shape
    gap_rows = 16 - 2 * width
    up = [(i, (i + 1) % lax.axis_size("gx")) for i in range(lax.axis_size("gx"))]
    down = [(j, i) for i, j in up]
    north = lax.ppermute(x[:, :, rows - width:], "gx", up)
    south = lax.ppermute(x[:, :, :width], "gx", down)
    gap = jnp.zeros((fields, levels, gap_rows, cols), x.dtype)
    tall = jnp.concatenate([x, south, gap, north], 2)
    right = [(i, i + 1) for i in range(lax.axis_size("gy") - 1)]
    left = [(j, i) for i, j in right]
    east = lax.ppermute(tall[..., :width], "gy", left)
    west = lax.ppermute(tall[..., cols - width:], "gy", right)
    middle = jnp.zeros((fields, levels, rows + 16, 128 - 2 * width), x.dtype)
    return jnp.concatenate([tall, east, middle, west], 3)


def diffusion_kernel(steps, rows, cols, v_ref, c_ref, o_ref):
    height, span = v_ref.shape[2], v_ref.shape[3]
    fields = o_ref.shape[0]
    along_i = c_ref[0, 0]
    along_j = c_ref[1, 0]
    sea = c_ref[2, 0]
    weight_i = along_i * sea * pltpu.roll(sea, height - 1, 0)
    weight_j = along_j * sea * pltpu.roll(sea, span - 1, 1)
    for f in range(fields):
        values = v_ref[f, 0]
        for s in range(steps):
            flux_i = weight_i * (pltpu.roll(values, height - 1, 0) - values)
            flux_j = weight_j * (pltpu.roll(values, span - 1, 1) - values)
            values = values + flux_i - pltpu.roll(flux_i, 1, 0) + flux_j - pltpu.roll(flux_j, 1, 1)
        o_ref[f, 0] = values[:rows, :cols]


def diffusion(values, coefs, steps):
    fields, levels, rows, cols = values.shape
    ext = circular(values, steps)
    height, span = ext.shape[2], ext.shape[3]
    return pl.pallas_call(
        functools.partial(diffusion_kernel, steps, rows, cols),
        out_shape=jax.ShapeDtypeStruct(values.shape, values.dtype),
        grid=(levels,),
        in_specs=[
            pl.BlockSpec((fields, 1, height, span), lambda l: (0, l, 0, 0)),
            pl.BlockSpec((coefs.shape[0], 1, height, span), lambda l: (0, l, 0, 0)),
        ],
        out_specs=pl.BlockSpec((fields, 1, rows, cols), lambda l: (0, l, 0, 0)),
    )(ext, coefs)


def lev_exchange(x, src_axis, dst_axis, half_axis, collective):
    n = lax.axis_size("lev")
    assert half_axis == src_axis
    out_shape = list(x.shape)
    out_shape[src_axis] //= n
    out_shape[dst_axis] *= n
    src_size = out_shape[src_axis]
    dst_size = x.shape[dst_axis]
    half = src_size // 2
    relay_shape = list(out_shape)
    relay_shape[dst_axis] = dst_size
    relay_shape[half_axis] = half

    def window(axis, start, size, h=None):
        index = [slice(None)] * x.ndim
        index[axis] = pl.ds(start, size)
        if h is not None:
            if half_axis == axis:
                index[axis] = pl.ds(start + h * half, half)
            else:
                index[half_axis] = pl.ds(h * half, half)
        return tuple(index)

    def kernel(x_ref, o_ref, relay, send_sem, recv_sem, local_sem):
        me = lax.axis_index("lev")
        gx = lax.axis_index("gx")
        gy = lax.axis_index("gy")
        right = (me + 1) % n
        left = (me + n - 1) % n
        opposite = (me + 2) % n
        barrier = pltpu.get_barrier_semaphore()
        for peer in (left, right):
            pl.semaphore_signal(barrier, inc=1, device_id=(peer, gx, gy), device_id_type=MESH)
        pl.semaphore_wait(barrier, 2)

        def remote(src, dst, slot, peer):
            return pltpu.make_async_remote_copy(
                src_ref=src, dst_ref=dst, send_sem=send_sem.at[slot], recv_sem=recv_sem.at[slot],
                device_id=(peer, gx, gy), device_id_type=MESH,
            )

        to_right = remote(x_ref.at[window(src_axis, right * src_size, src_size)],
                          o_ref.at[window(dst_axis, me * dst_size, dst_size)], 0, right)
        to_left = remote(x_ref.at[window(src_axis, left * src_size, src_size)],
                         o_ref.at[window(dst_axis, me * dst_size, dst_size)], 1, left)
        via_right = remote(x_ref.at[window(src_axis, opposite * src_size, src_size, 0)], relay.at[0], 2, right)
        via_left = remote(x_ref.at[window(src_axis, opposite * src_size, src_size, 1)], relay.at[1], 3, left)
        for copy in (via_right, via_left, to_right, to_left):
            copy.start()
        local = pltpu.make_async_copy(
            x_ref.at[window(src_axis, me * src_size, src_size)],
            o_ref.at[window(dst_axis, me * dst_size, dst_size)],
            local_sem,
        )
        local.start()
        via_right.wait_recv()
        on_right = remote(relay.at[0], o_ref.at[window(dst_axis, left * dst_size, dst_size, 0)], 4, right)
        on_right.start()
        via_left.wait_recv()
        on_left = remote(relay.at[1], o_ref.at[window(dst_axis, right * dst_size, dst_size, 1)], 5, left)
        on_left.start()
        local.wait()
        via_right.wait_send()
        via_left.wait_send()
        for copy in (to_right, to_left, on_right, on_left):
            copy.wait()

    return pl.pallas_call(
        kernel,
        out_shape=jax.ShapeDtypeStruct(tuple(out_shape), x.dtype),
        in_specs=[pl.BlockSpec(memory_space=pl.ANY)],
        out_specs=pl.BlockSpec(memory_space=pl.ANY),
        scratch_shapes=[
            pltpu.VMEM((2,) + tuple(relay_shape), x.dtype),
            pltpu.SemaphoreType.DMA((6,)),
            pltpu.SemaphoreType.DMA((6,)),
            pltpu.SemaphoreType.DMA,
        ],
        compiler_params=pltpu.CompilerParams(collective_id=collective, has_side_effects=True),
    )(x)


def to_columns(x, kernel=True):
    if kernel:
        return lev_exchange(x, 2, 1, 2, 0)
    return lax.all_to_all(x, "lev", 2, 1, tiled=True)


def to_levels(x, kernel=True):
    if kernel:
        return lev_exchange(x, 1, 2, 1, 1)
    return lax.all_to_all(x, "lev", 1, 2, tiled=True)


def level_mix(fields, matrix):
    columns = to_columns(fields)
    mixed = jnp.einsum("abcd,cdij->abij", matrix, columns, precision=lax.Precision.HIGHEST)
    return to_levels(mixed)


def shards(increment, norm_gain, diffusion_i, diffusion_j, sea_mask, coupling):
    steps = 2 * ITERS
    ocean = sea_mask.astype(jnp.float32)
    scaled = ocean[None] * norm_gain * increment
    order_count = coupling.shape[0]
    level_count = order_count // 2
    balance = jnp.eye(order_count, dtype=jnp.float32) + coupling
    forward = balance.reshape(2, level_count, 2, level_count)
    adjoint = jnp.transpose(forward, (2, 3, 0, 1))
    coefs = circular(jnp.stack([diffusion_i, diffusion_j, ocean]), steps)
    columns = to_columns(scaled, False)
    mixed = jnp.einsum("abcd,cdij->abij", adjoint, columns, precision=lax.Precision.HIGHEST)
    coefs, mixed = lax.optimization_barrier((coefs, mixed))
    adjoint_mixed = to_levels(mixed) * ocean[None]
    spread = diffusion(adjoint_mixed, coefs, steps)
    forward_mixed = level_mix(spread, forward)
    return ocean[None] * norm_gain * forward_mixed


def solution(mesh):
    return jax.shard_map(
        shards,
        mesh=mesh,
        in_specs=(
            P(None, "lev", "gx", "gy"),
            P(None, "lev", "gx", "gy"),
            P("lev", "gx", "gy"),
            P("lev", "gx", "gy"),
            P("lev", "gx", "gy"),
            P(),
        ),
        out_specs=P(None, "lev", "gx", "gy"),
        check_vma=False,
    )
```

```python
import functools

import jax
import jax.numpy as jnp
from jax import lax
from jax.experimental import pallas as pl
from jax.experimental.pallas import tpu as pltpu
from jax.sharding import PartitionSpec as P

ITERS = 2
MESH = pl.DeviceIdType.MESH


def circular(x, width):
    fields, levels, rows, cols = x.shape
    gap_rows = 16 - 2 * width
    up = [(i, (i + 1) % lax.axis_size("gx")) for i in range(lax.axis_size("gx"))]
    down = [(j, i) for i, j in up]
    north = lax.ppermute(x[:, :, rows - width:], "gx", up)
    south = lax.ppermute(x[:, :, :width], "gx", down)
    gap = jnp.zeros((fields, levels, gap_rows, cols), x.dtype)
    tall = jnp.concatenate([x, south, gap, north], 2)
    right = [(i, i + 1) for i in range(lax.axis_size("gy") - 1)]
    left = [(j, i) for i, j in right]
    east = lax.ppermute(tall[..., :width], "gy", left)
    west = lax.ppermute(tall[..., cols - width:], "gy", right)
    middle = jnp.zeros((fields, levels, rows + 16, 128 - 2 * width), x.dtype)
    return jnp.concatenate([tall, east, middle, west], 3)


def diffusion_kernel(steps, rows, cols, v_ref, c_ref, o_ref):
    height, span = v_ref.shape[2], v_ref.shape[3]
    fields = o_ref.shape[0]
    along_i = c_ref[0, 0]
    along_j = c_ref[1, 0]
    sea = c_ref[2, 0]
    weight_i = along_i * sea * pltpu.roll(sea, height - 1, 0)
    weight_j = along_j * sea * pltpu.roll(sea, span - 1, 1)
    for f in range(fields):
        values = v_ref[f, 0]
        for s in range(steps):
            flux_i = weight_i * (pltpu.roll(values, height - 1, 0) - values)
            flux_j = weight_j * (pltpu.roll(values, span - 1, 1) - values)
            values = values + flux_i - pltpu.roll(flux_i, 1, 0) + flux_j - pltpu.roll(flux_j, 1, 1)
        o_ref[f, 0] = values[:rows, :cols]


def diffusion(values, coefs, steps):
    fields, levels, rows, cols = values.shape
    ext = circular(values, steps)
    height, span = ext.shape[2], ext.shape[3]
    return pl.pallas_call(
        functools.partial(diffusion_kernel, steps, rows, cols),
        out_shape=jax.ShapeDtypeStruct(values.shape, values.dtype),
        grid=(levels,),
        in_specs=[
            pl.BlockSpec((fields, 1, height, span), lambda l: (0, l, 0, 0)),
            pl.BlockSpec((coefs.shape[0], 1, height, span), lambda l: (0, l, 0, 0)),
        ],
        out_specs=pl.BlockSpec((fields, 1, rows, cols), lambda l: (0, l, 0, 0)),
    )(ext, coefs)


def lev_exchange(x, src_axis, dst_axis, half_axis, collective):
    n = lax.axis_size("lev")
    assert half_axis == src_axis
    out_shape = list(x.shape)
    out_shape[src_axis] //= n
    out_shape[dst_axis] *= n
    src_size = out_shape[src_axis]
    dst_size = x.shape[dst_axis]
    half = src_size // 2
    relay_shape = list(out_shape)
    relay_shape[dst_axis] = dst_size
    relay_shape[half_axis] = half

    def window(axis, start, size, h=None):
        index = [slice(None)] * x.ndim
        index[axis] = pl.ds(start, size)
        if h is not None:
            if half_axis == axis:
                index[axis] = pl.ds(start + h * half, half)
            else:
                index[half_axis] = pl.ds(h * half, half)
        return tuple(index)

    def kernel(x_ref, o_ref, relay, send_sem, recv_sem, local_sem):
        me = lax.axis_index("lev")
        gx = lax.axis_index("gx")
        gy = lax.axis_index("gy")
        right = (me + 1) % n
        left = (me + n - 1) % n
        opposite = (me + 2) % n
        barrier = pltpu.get_barrier_semaphore()
        for peer in (left, right):
            pl.semaphore_signal(barrier, inc=1, device_id=(peer, gx, gy), device_id_type=MESH)
        pl.semaphore_wait(barrier, 2)

        def remote(src, dst, slot, peer):
            return pltpu.make_async_remote_copy(
                src_ref=src, dst_ref=dst, send_sem=send_sem.at[slot], recv_sem=recv_sem.at[slot],
                device_id=(peer, gx, gy), device_id_type=MESH,
            )

        to_right = remote(x_ref.at[window(src_axis, right * src_size, src_size)],
                          o_ref.at[window(dst_axis, me * dst_size, dst_size)], 0, right)
        to_left = remote(x_ref.at[window(src_axis, left * src_size, src_size)],
                         o_ref.at[window(dst_axis, me * dst_size, dst_size)], 1, left)
        via_right = remote(x_ref.at[window(src_axis, opposite * src_size, src_size, 0)], relay.at[0], 2, right)
        via_left = remote(x_ref.at[window(src_axis, opposite * src_size, src_size, 1)], relay.at[1], 3, left)
        for copy in (via_right, via_left, to_right, to_left):
            copy.start()
        local = pltpu.make_async_copy(
            x_ref.at[window(src_axis, me * src_size, src_size)],
            o_ref.at[window(dst_axis, me * dst_size, dst_size)],
            local_sem,
        )
        local.start()
        via_right.wait_recv()
        on_right = remote(relay.at[0], o_ref.at[window(dst_axis, left * dst_size, dst_size, 0)], 4, right)
        on_right.start()
        via_left.wait_recv()
        on_left = remote(relay.at[1], o_ref.at[window(dst_axis, right * dst_size, dst_size, 1)], 5, left)
        on_left.start()
        local.wait()
        via_right.wait_send()
        via_left.wait_send()
        for copy in (to_right, to_left, on_right, on_left):
            copy.wait()

    return pl.pallas_call(
        kernel,
        out_shape=jax.ShapeDtypeStruct(tuple(out_shape), x.dtype),
        in_specs=[pl.BlockSpec(memory_space=pl.ANY)],
        out_specs=pl.BlockSpec(memory_space=pl.ANY),
        scratch_shapes=[
            pltpu.VMEM((2,) + tuple(relay_shape), x.dtype),
            pltpu.SemaphoreType.DMA((6,)),
            pltpu.SemaphoreType.DMA((6,)),
            pltpu.SemaphoreType.DMA,
        ],
        compiler_params=pltpu.CompilerParams(collective_id=collective, has_side_effects=True),
    )(x)


def to_columns(x, kernel=True):
    if kernel:
        return lev_exchange(x, 2, 1, 2, 0)
    return lax.all_to_all(x, "lev", 2, 1, tiled=True)


def to_levels(x, kernel=True):
    if kernel:
        return lev_exchange(x, 1, 2, 1, 1)
    return lax.all_to_all(x, "lev", 1, 2, tiled=True)


def level_mix(fields, matrix):
    columns = to_columns(fields)
    mixed = jnp.einsum("abcd,cdij->abij", matrix, columns, precision=lax.Precision.HIGHEST)
    return to_levels(mixed)


def shards(increment, norm_gain, diffusion_i, diffusion_j, sea_mask, coupling):
    steps = 2 * ITERS
    ocean = sea_mask.astype(jnp.float32)
    scaled = ocean[None] * norm_gain * increment
    order_count = coupling.shape[0]
    level_count = order_count // 2
    balance = jnp.eye(order_count, dtype=jnp.float32) + coupling
    forward = balance.reshape(2, level_count, 2, level_count)
    adjoint = jnp.transpose(forward, (2, 3, 0, 1))
    columns = to_columns(scaled)
    coefs, columns = lax.optimization_barrier((jnp.stack([diffusion_i, diffusion_j, ocean]), columns))
    coefs = circular(coefs, steps)
    mixed = jnp.einsum("abcd,cdij->abij", adjoint, columns, precision=lax.Precision.HIGHEST)
    adjoint_mixed = to_levels(mixed, False) * ocean[None]
    spread = diffusion(adjoint_mixed, coefs, steps)
    forward_mixed = level_mix(spread, forward)
    return ocean[None] * norm_gain * forward_mixed


def solution(mesh):
    return jax.shard_map(
        shards,
        mesh=mesh,
        in_specs=(
            P(None, "lev", "gx", "gy"),
            P(None, "lev", "gx", "gy"),
            P("lev", "gx", "gy"),
            P("lev", "gx", "gy"),
            P("lev", "gx", "gy"),
            P(),
        ),
        out_specs=P(None, "lev", "gx", "gy"),
        check_vma=False,
    )
```

```python
import functools

import jax
import jax.numpy as jnp
from jax import lax
from jax.experimental import pallas as pl
from jax.experimental.pallas import tpu as pltpu
from jax.sharding import PartitionSpec as P

ITERS = 2
MESH = pl.DeviceIdType.MESH


def pieces(x, height, width):
    fields, levels, rows, cols = x.shape
    up = [(i, (i + 1) % lax.axis_size("gx")) for i in range(lax.axis_size("gx"))]
    down = [(j, i) for i, j in up]
    north = lax.ppermute(x[:, :, rows - height:], "gx", up)
    south = lax.ppermute(x[:, :, :height], "gx", down)
    tall = jnp.concatenate([x, south, north], 2)
    right = [(i, i + 1) for i in range(lax.axis_size("gy") - 1)]
    left = [(j, i) for i, j in right]
    east = lax.ppermute(tall[..., :width], "gy", left)
    west = lax.ppermute(tall[..., cols - width:], "gy", right)
    middle = jnp.zeros((fields, levels, rows + 2 * height, 128 - 2 * width), x.dtype)
    edge = jnp.concatenate([east, middle, west], 3)
    return tall, south, north, edge


def circular(x, height, width):
    tall, _, _, edge = pieces(x, height, width)
    return jnp.concatenate([tall, edge], 3)


def diffusion_kernel(steps, rows, cols, x_ref, s_ref, n_ref, e_ref, c_ref, o_ref):
    height, span = c_ref.shape[2], c_ref.shape[3]
    fields = o_ref.shape[0]
    along_i = c_ref[0, 0]
    along_j = c_ref[1, 0]
    sea = c_ref[2, 0]
    weight_i = along_i * sea * pltpu.roll(sea, height - 1, 0)
    weight_j = along_j * sea * pltpu.roll(sea, span - 1, 1)
    for f in range(fields):
        values = jnp.concatenate(
            [jnp.concatenate([x_ref[f, 0], s_ref[f, 0], n_ref[f, 0]], 0), e_ref[f, 0]], 1
        )
        for s in range(steps):
            flux_i = weight_i * (pltpu.roll(values, height - 1, 0) - values)
            flux_j = weight_j * (pltpu.roll(values, span - 1, 1) - values)
            values = values + flux_i - pltpu.roll(flux_i, 1, 0) + flux_j - pltpu.roll(flux_j, 1, 1)
        o_ref[f, 0] = values[:rows, :cols]


def diffusion(values, coefs, steps):
    fields, levels, rows, cols = values.shape
    _, south, north, edge = pieces(values, 2 * steps, steps)
    height, span = coefs.shape[2], coefs.shape[3]
    band = south.shape[2]
    return pl.pallas_call(
        functools.partial(diffusion_kernel, steps, rows, cols),
        out_shape=jax.ShapeDtypeStruct(values.shape, values.dtype),
        grid=(levels,),
        in_specs=[
            pl.BlockSpec((fields, 1, rows, cols), lambda l: (0, l, 0, 0)),
            pl.BlockSpec((fields, 1, band, cols), lambda l: (0, l, 0, 0)),
            pl.BlockSpec((fields, 1, band, cols), lambda l: (0, l, 0, 0)),
            pl.BlockSpec((fields, 1, height, 128), lambda l: (0, l, 0, 0)),
            pl.BlockSpec((coefs.shape[0], 1, height, span), lambda l: (0, l, 0, 0)),
        ],
        out_specs=pl.BlockSpec((fields, 1, rows, cols), lambda l: (0, l, 0, 0)),
    )(values, south, north, edge, coefs)


def lev_exchange(x, src_axis, dst_axis, half_axis, collective):
    n = lax.axis_size("lev")
    assert half_axis == src_axis
    out_shape = list(x.shape)
    out_shape[src_axis] //= n
    out_shape[dst_axis] *= n
    src_size = out_shape[src_axis]
    dst_size = x.shape[dst_axis]
    half = src_size // 2
    relay_shape = list(out_shape)
    relay_shape[dst_axis] = dst_size
    relay_shape[half_axis] = half

    def window(axis, start, size, h=None):
        index = [slice(None)] * x.ndim
        index[axis] = pl.ds(start, size)
        if h is not None:
            if half_axis == axis:
                index[axis] = pl.ds(start + h * half, half)
            else:
                index[half_axis] = pl.ds(h * half, half)
        return tuple(index)

    def kernel(x_ref, o_ref, relay, send_sem, recv_sem, local_sem):
        me = lax.axis_index("lev")
        gx = lax.axis_index("gx")
        gy = lax.axis_index("gy")
        right = (me + 1) % n
        left = (me + n - 1) % n
        opposite = (me + 2) % n
        barrier = pltpu.get_barrier_semaphore()
        for peer in (left, right):
            pl.semaphore_signal(barrier, inc=1, device_id=(peer, gx, gy), device_id_type=MESH)
        pl.semaphore_wait(barrier, 2)

        def remote(src, dst, slot, peer):
            return pltpu.make_async_remote_copy(
                src_ref=src, dst_ref=dst, send_sem=send_sem.at[slot], recv_sem=recv_sem.at[slot],
                device_id=(peer, gx, gy), device_id_type=MESH,
            )

        to_right = remote(x_ref.at[window(src_axis, right * src_size, src_size)],
                          o_ref.at[window(dst_axis, me * dst_size, dst_size)], 0, right)
        to_left = remote(x_ref.at[window(src_axis, left * src_size, src_size)],
                         o_ref.at[window(dst_axis, me * dst_size, dst_size)], 1, left)
        via_right = remote(x_ref.at[window(src_axis, opposite * src_size, src_size, 0)], relay.at[0], 2, right)
        via_left = remote(x_ref.at[window(src_axis, opposite * src_size, src_size, 1)], relay.at[1], 3, left)
        for copy in (via_right, via_left, to_right, to_left):
            copy.start()
        local = pltpu.make_async_copy(
            x_ref.at[window(src_axis, me * src_size, src_size)],
            o_ref.at[window(dst_axis, me * dst_size, dst_size)],
            local_sem,
        )
        local.start()
        via_right.wait_recv()
        on_right = remote(relay.at[0], o_ref.at[window(dst_axis, left * dst_size, dst_size, 0)], 4, right)
        on_right.start()
        via_left.wait_recv()
        on_left = remote(relay.at[1], o_ref.at[window(dst_axis, right * dst_size, dst_size, 1)], 5, left)
        on_left.start()
        local.wait()
        via_right.wait_send()
        via_left.wait_send()
        for copy in (to_right, to_left, on_right, on_left):
            copy.wait()

    return pl.pallas_call(
        kernel,
        out_shape=jax.ShapeDtypeStruct(tuple(out_shape), x.dtype),
        in_specs=[pl.BlockSpec(memory_space=pl.ANY)],
        out_specs=pl.BlockSpec(memory_space=pl.ANY),
        scratch_shapes=[
            pltpu.VMEM((2,) + tuple(relay_shape), x.dtype),
            pltpu.SemaphoreType.DMA((6,)),
            pltpu.SemaphoreType.DMA((6,)),
            pltpu.SemaphoreType.DMA,
        ],
        compiler_params=pltpu.CompilerParams(collective_id=collective, has_side_effects=True),
    )(x)


def to_columns(x, kernel=True):
    if kernel:
        return lev_exchange(x, 2, 1, 2, 0)
    return lax.all_to_all(x, "lev", 2, 1, tiled=True)


def to_levels(x, kernel=True):
    if kernel:
        return lev_exchange(x, 1, 2, 1, 1)
    return lax.all_to_all(x, "lev", 1, 2, tiled=True)


def level_mix(fields, matrix):
    columns = to_columns(fields)
    mixed = jnp.einsum("abcd,cdij->abij", matrix, columns, precision=lax.Precision.HIGHEST)
    return to_levels(mixed)


def shards(increment, norm_gain, diffusion_i, diffusion_j, sea_mask, coupling):
    steps = 2 * ITERS
    ocean = sea_mask.astype(jnp.float32)
    scaled = ocean[None] * norm_gain * increment
    order_count = coupling.shape[0]
    level_count = order_count // 2
    balance = jnp.eye(order_count, dtype=jnp.float32) + coupling
    forward = balance.reshape(2, level_count, 2, level_count)
    adjoint = jnp.transpose(forward, (2, 3, 0, 1))
    coefs = circular(jnp.stack([diffusion_i, diffusion_j, ocean]), 2 * steps, steps)
    columns = to_columns(scaled, False)
    mixed = jnp.einsum("abcd,cdij->abij", adjoint, columns, precision=lax.Precision.HIGHEST)
    coefs, mixed = lax.optimization_barrier((coefs, mixed))
    adjoint_mixed = to_levels(mixed) * ocean[None]
    spread = diffusion(adjoint_mixed, coefs, steps)
    forward_mixed = level_mix(spread, forward)
    return ocean[None] * norm_gain * forward_mixed


def solution(mesh):
    return jax.shard_map(
        shards,
        mesh=mesh,
        in_specs=(
            P(None, "lev", "gx", "gy"),
            P(None, "lev", "gx", "gy"),
            P("lev", "gx", "gy"),
            P("lev", "gx", "gy"),
            P("lev", "gx", "gy"),
            P(),
        ),
        out_specs=P(None, "lev", "gx", "gy"),
        check_vma=False,
    )
```

```python
import functools

import jax
import jax.numpy as jnp
from jax import lax
from jax.experimental import pallas as pl
from jax.experimental.pallas import tpu as pltpu
from jax.sharding import PartitionSpec as P

ITERS = 2
MESH = pl.DeviceIdType.MESH


def pieces(x, height, width):
    fields, levels, rows, cols = x.shape
    up = [(i, (i + 1) % lax.axis_size("gx")) for i in range(lax.axis_size("gx"))]
    down = [(j, i) for i, j in up]
    north = lax.ppermute(x[:, :, rows - height:], "gx", up)
    south = lax.ppermute(x[:, :, :height], "gx", down)
    tall = jnp.concatenate([x, south, north], 2)
    right = [(i, i + 1) for i in range(lax.axis_size("gy") - 1)]
    left = [(j, i) for i, j in right]
    east = lax.ppermute(tall[..., :width], "gy", left)
    west = lax.ppermute(tall[..., cols - width:], "gy", right)
    middle = jnp.zeros((fields, levels, rows + 2 * height, 128 - 2 * width), x.dtype)
    edge = jnp.concatenate([east, middle, west], 3)
    return tall, south, north, edge


def circular(x, height, width):
    tall, _, _, edge = pieces(x, height, width)
    return jnp.concatenate([tall, edge], 3)


def plane(t_ref, s_ref, n_ref, e_ref, f):
    tall = jnp.concatenate([t_ref[f, 0], s_ref[f, 0], n_ref[f, 0]], 0)
    return jnp.concatenate([tall, e_ref[f, 0]], 1)


def diffusion_kernel(steps, rows, cols, x_ref, s_ref, n_ref, e_ref, ct_ref, cs_ref, cn_ref, ce_ref, o_ref):
    height, span = e_ref.shape[2], 2 * e_ref.shape[3]
    fields = o_ref.shape[0]
    along_i = plane(ct_ref, cs_ref, cn_ref, ce_ref, 0)
    along_j = plane(ct_ref, cs_ref, cn_ref, ce_ref, 1)
    sea = plane(ct_ref, cs_ref, cn_ref, ce_ref, 2)
    weight_i = along_i * sea * pltpu.roll(sea, height - 1, 0)
    weight_j = along_j * sea * pltpu.roll(sea, span - 1, 1)
    for f in range(fields):
        values = plane(x_ref, s_ref, n_ref, e_ref, f)
        for s in range(steps):
            flux_i = weight_i * (pltpu.roll(values, height - 1, 0) - values)
            flux_j = weight_j * (pltpu.roll(values, span - 1, 1) - values)
            values = values + flux_i - pltpu.roll(flux_i, 1, 0) + flux_j - pltpu.roll(flux_j, 1, 1)
        o_ref[f, 0] = values[:rows, :cols]


def diffusion(values, coefs, steps):
    fields, levels, rows, cols = values.shape
    height = rows + 4 * steps
    band = 2 * steps

    def specs(channels):
        return [
            pl.BlockSpec((channels, 1, rows, cols), lambda l: (0, l, 0, 0)),
            pl.BlockSpec((channels, 1, band, cols), lambda l: (0, l, 0, 0)),
            pl.BlockSpec((channels, 1, band, cols), lambda l: (0, l, 0, 0)),
            pl.BlockSpec((channels, 1, height, 128), lambda l: (0, l, 0, 0)),
        ]

    _, south, north, edge = pieces(values, band, steps)
    _, coef_south, coef_north, coef_edge = coefs
    return pl.pallas_call(
        functools.partial(diffusion_kernel, steps, rows, cols),
        out_shape=jax.ShapeDtypeStruct(values.shape, values.dtype),
        grid=(levels,),
        in_specs=specs(fields) + specs(coef_edge.shape[0]),
        out_specs=pl.BlockSpec((fields, 1, rows, cols), lambda l: (0, l, 0, 0)),
    )(values, south, north, edge, coefs[0], coef_south, coef_north, coef_edge)


def lev_exchange(x, src_axis, dst_axis, half_axis, collective):
    n = lax.axis_size("lev")
    assert half_axis == src_axis
    out_shape = list(x.shape)
    out_shape[src_axis] //= n
    out_shape[dst_axis] *= n
    src_size = out_shape[src_axis]
    dst_size = x.shape[dst_axis]
    half = src_size // 2
    relay_shape = list(out_shape)
    relay_shape[dst_axis] = dst_size
    relay_shape[half_axis] = half

    def window(axis, start, size, h=None):
        index = [slice(None)] * x.ndim
        index[axis] = pl.ds(start, size)
        if h is not None:
            if half_axis == axis:
                index[axis] = pl.ds(start + h * half, half)
            else:
                index[half_axis] = pl.ds(h * half, half)
        return tuple(index)

    def kernel(x_ref, o_ref, relay, send_sem, recv_sem, local_sem):
        me = lax.axis_index("lev")
        gx = lax.axis_index("gx")
        gy = lax.axis_index("gy")
        right = (me + 1) % n
        left = (me + n - 1) % n
        opposite = (me + 2) % n
        barrier = pltpu.get_barrier_semaphore()
        for peer in (left, right):
            pl.semaphore_signal(barrier, inc=1, device_id=(peer, gx, gy), device_id_type=MESH)
        pl.semaphore_wait(barrier, 2)

        def remote(src, dst, slot, peer):
            return pltpu.make_async_remote_copy(
                src_ref=src, dst_ref=dst, send_sem=send_sem.at[slot], recv_sem=recv_sem.at[slot],
                device_id=(peer, gx, gy), device_id_type=MESH,
            )

        to_right = remote(x_ref.at[window(src_axis, right * src_size, src_size)],
                          o_ref.at[window(dst_axis, me * dst_size, dst_size)], 0, right)
        to_left = remote(x_ref.at[window(src_axis, left * src_size, src_size)],
                         o_ref.at[window(dst_axis, me * dst_size, dst_size)], 1, left)
        via_right = remote(x_ref.at[window(src_axis, opposite * src_size, src_size, 0)], relay.at[0], 2, right)
        via_left = remote(x_ref.at[window(src_axis, opposite * src_size, src_size, 1)], relay.at[1], 3, left)
        for copy in (via_right, via_left, to_right, to_left):
            copy.start()
        local = pltpu.make_async_copy(
            x_ref.at[window(src_axis, me * src_size, src_size)],
            o_ref.at[window(dst_axis, me * dst_size, dst_size)],
            local_sem,
        )
        local.start()
        via_right.wait_recv()
        on_right = remote(relay.at[0], o_ref.at[window(dst_axis, left * dst_size, dst_size, 0)], 4, right)
        on_right.start()
        via_left.wait_recv()
        on_left = remote(relay.at[1], o_ref.at[window(dst_axis, right * dst_size, dst_size, 1)], 5, left)
        on_left.start()
        local.wait()
        via_right.wait_send()
        via_left.wait_send()
        for copy in (to_right, to_left, on_right, on_left):
            copy.wait()

    return pl.pallas_call(
        kernel,
        out_shape=jax.ShapeDtypeStruct(tuple(out_shape), x.dtype),
        in_specs=[pl.BlockSpec(memory_space=pl.ANY)],
        out_specs=pl.BlockSpec(memory_space=pl.ANY),
        scratch_shapes=[
            pltpu.VMEM((2,) + tuple(relay_shape), x.dtype),
            pltpu.SemaphoreType.DMA((6,)),
            pltpu.SemaphoreType.DMA((6,)),
            pltpu.SemaphoreType.DMA,
        ],
        compiler_params=pltpu.CompilerParams(collective_id=collective, has_side_effects=True),
    )(x)


def to_columns(x, kernel=True):
    if kernel:
        return lev_exchange(x, 2, 1, 2, 0)
    return lax.all_to_all(x, "lev", 2, 1, tiled=True)


def to_levels(x, kernel=True):
    if kernel:
        return lev_exchange(x, 1, 2, 1, 1)
    return lax.all_to_all(x, "lev", 1, 2, tiled=True)


def level_mix(fields, matrix):
    columns = to_columns(fields)
    mixed = jnp.einsum("abcd,cdij->abij", matrix, columns, precision=lax.Precision.HIGHEST)
    return to_levels(mixed)


def shards(increment, norm_gain, diffusion_i, diffusion_j, sea_mask, coupling):
    steps = 2 * ITERS
    ocean = sea_mask.astype(jnp.float32)
    scaled = ocean[None] * norm_gain * increment
    order_count = coupling.shape[0]
    level_count = order_count // 2
    balance = jnp.eye(order_count, dtype=jnp.float32) + coupling
    forward = balance.reshape(2, level_count, 2, level_count)
    adjoint = jnp.transpose(forward, (2, 3, 0, 1))
    stacked = jnp.stack([diffusion_i, diffusion_j, ocean])
    coefs = (stacked,) + pieces(stacked, 2 * steps, steps)[1:]
    columns = to_columns(scaled, False)
    mixed = jnp.einsum("abcd,cdij->abij", adjoint, columns, precision=lax.Precision.HIGHEST)
    coefs, mixed = lax.optimization_barrier((coefs, mixed))
    adjoint_mixed = to_levels(mixed) * ocean[None]
    spread = diffusion(adjoint_mixed, coefs, steps)
    forward_mixed = level_mix(spread, forward)
    return ocean[None] * norm_gain * forward_mixed


def solution(mesh):
    return jax.shard_map(
        shards,
        mesh=mesh,
        in_specs=(
            P(None, "lev", "gx", "gy"),
            P(None, "lev", "gx", "gy"),
            P("lev", "gx", "gy"),
            P("lev", "gx", "gy"),
            P("lev", "gx", "gy"),
            P(),
        ),
        out_specs=P(None, "lev", "gx", "gy"),
        check_vma=False,
    )
```

```python
import functools

import jax
import jax.numpy as jnp
from jax import lax
from jax.experimental import pallas as pl
from jax.experimental.pallas import tpu as pltpu
from jax.sharding import PartitionSpec as P

ITERS = 2
MESH = pl.DeviceIdType.MESH


def pieces(x, height, width):
    fields, levels, rows, cols = x.shape
    up = [(i, (i + 1) % lax.axis_size("gx")) for i in range(lax.axis_size("gx"))]
    down = [(j, i) for i, j in up]
    north = lax.ppermute(x[:, :, rows - height:], "gx", up)
    south = lax.ppermute(x[:, :, :height], "gx", down)
    tall = jnp.concatenate([x, south, north], 2)
    right = [(i, i + 1) for i in range(lax.axis_size("gy") - 1)]
    left = [(j, i) for i, j in right]
    east = lax.ppermute(tall[..., :width], "gy", left)
    west = lax.ppermute(tall[..., cols - width:], "gy", right)
    middle = jnp.zeros((fields, levels, rows + 2 * height, 128 - 2 * width), x.dtype)
    edge = jnp.concatenate([east, middle, west], 3)
    return tall, south, north, edge


def circular(x, height, width):
    tall, _, _, edge = pieces(x, height, width)
    return jnp.concatenate([tall, edge], 3)


def plane(t_ref, s_ref, n_ref, e_ref, f):
    tall = jnp.concatenate([t_ref[f, 0], s_ref[f, 0], n_ref[f, 0]], 0)
    return jnp.concatenate([tall, e_ref[f, 0]], 1)


def diffusion_kernel(steps, rows, cols, x_ref, s_ref, n_ref, e_ref, ct_ref, cs_ref, cn_ref, ce_ref, o_ref):
    height, span = e_ref.shape[2], 2 * e_ref.shape[3]
    fields = o_ref.shape[0]
    along_i = plane(ct_ref, cs_ref, cn_ref, ce_ref, 0)
    along_j = plane(ct_ref, cs_ref, cn_ref, ce_ref, 1)
    sea = plane(ct_ref, cs_ref, cn_ref, ce_ref, 2)
    weight_i = along_i * sea * pltpu.roll(sea, height - 1, 0)
    weight_j = along_j * sea * pltpu.roll(sea, span - 1, 1)
    for f in range(fields):
        values = plane(x_ref, s_ref, n_ref, e_ref, f) * sea
        for s in range(steps):
            flux_i = weight_i * (pltpu.roll(values, height - 1, 0) - values)
            flux_j = weight_j * (pltpu.roll(values, span - 1, 1) - values)
            values = values + flux_i - pltpu.roll(flux_i, 1, 0) + flux_j - pltpu.roll(flux_j, 1, 1)
        o_ref[f, 0] = values[:rows, :cols]


def diffusion(values, coefs, steps):
    fields, levels, rows, cols = values.shape
    height = rows + 4 * steps
    band = 2 * steps

    def specs(channels):
        return [
            pl.BlockSpec((channels, 1, rows, cols), lambda l: (0, l, 0, 0)),
            pl.BlockSpec((channels, 1, band, cols), lambda l: (0, l, 0, 0)),
            pl.BlockSpec((channels, 1, band, cols), lambda l: (0, l, 0, 0)),
            pl.BlockSpec((channels, 1, height, 128), lambda l: (0, l, 0, 0)),
        ]

    _, south, north, edge = pieces(values, band, steps)
    _, coef_south, coef_north, coef_edge = coefs
    return pl.pallas_call(
        functools.partial(diffusion_kernel, steps, rows, cols),
        out_shape=jax.ShapeDtypeStruct(values.shape, values.dtype),
        grid=(levels,),
        in_specs=specs(fields) + specs(coef_edge.shape[0]),
        out_specs=pl.BlockSpec((fields, 1, rows, cols), lambda l: (0, l, 0, 0)),
    )(values, south, north, edge, coefs[0], coef_south, coef_north, coef_edge)


def lev_exchange(x, src_axis, dst_axis, half_axis, collective):
    n = lax.axis_size("lev")
    assert half_axis == src_axis
    out_shape = list(x.shape)
    out_shape[src_axis] //= n
    out_shape[dst_axis] *= n
    src_size = out_shape[src_axis]
    dst_size = x.shape[dst_axis]
    half = src_size // 2
    relay_shape = list(out_shape)
    relay_shape[dst_axis] = dst_size
    relay_shape[half_axis] = half

    def window(axis, start, size, h=None):
        index = [slice(None)] * x.ndim
        index[axis] = pl.ds(start, size)
        if h is not None:
            if half_axis == axis:
                index[axis] = pl.ds(start + h * half, half)
            else:
                index[half_axis] = pl.ds(h * half, half)
        return tuple(index)

    def kernel(x_ref, o_ref, relay, send_sem, recv_sem, local_sem):
        me = lax.axis_index("lev")
        gx = lax.axis_index("gx")
        gy = lax.axis_index("gy")
        right = (me + 1) % n
        left = (me + n - 1) % n
        opposite = (me + 2) % n
        barrier = pltpu.get_barrier_semaphore()
        for peer in (left, right):
            pl.semaphore_signal(barrier, inc=1, device_id=(peer, gx, gy), device_id_type=MESH)
        pl.semaphore_wait(barrier, 2)

        def remote(src, dst, slot, peer):
            return pltpu.make_async_remote_copy(
                src_ref=src, dst_ref=dst, send_sem=send_sem.at[slot], recv_sem=recv_sem.at[slot],
                device_id=(peer, gx, gy), device_id_type=MESH,
            )

        to_right = remote(x_ref.at[window(src_axis, right * src_size, src_size)],
                          o_ref.at[window(dst_axis, me * dst_size, dst_size)], 0, right)
        to_left = remote(x_ref.at[window(src_axis, left * src_size, src_size)],
                         o_ref.at[window(dst_axis, me * dst_size, dst_size)], 1, left)
        via_right = remote(x_ref.at[window(src_axis, opposite * src_size, src_size, 0)], relay.at[0], 2, right)
        via_left = remote(x_ref.at[window(src_axis, opposite * src_size, src_size, 1)], relay.at[1], 3, left)
        for copy in (via_right, via_left, to_right, to_left):
            copy.start()
        local = pltpu.make_async_copy(
            x_ref.at[window(src_axis, me * src_size, src_size)],
            o_ref.at[window(dst_axis, me * dst_size, dst_size)],
            local_sem,
        )
        local.start()
        via_right.wait_recv()
        on_right = remote(relay.at[0], o_ref.at[window(dst_axis, left * dst_size, dst_size, 0)], 4, right)
        on_right.start()
        via_left.wait_recv()
        on_left = remote(relay.at[1], o_ref.at[window(dst_axis, right * dst_size, dst_size, 1)], 5, left)
        on_left.start()
        local.wait()
        via_right.wait_send()
        via_left.wait_send()
        for copy in (to_right, to_left, on_right, on_left):
            copy.wait()

    return pl.pallas_call(
        kernel,
        out_shape=jax.ShapeDtypeStruct(tuple(out_shape), x.dtype),
        in_specs=[pl.BlockSpec(memory_space=pl.ANY)],
        out_specs=pl.BlockSpec(memory_space=pl.ANY),
        scratch_shapes=[
            pltpu.VMEM((2,) + tuple(relay_shape), x.dtype),
            pltpu.SemaphoreType.DMA((6,)),
            pltpu.SemaphoreType.DMA((6,)),
            pltpu.SemaphoreType.DMA,
        ],
        compiler_params=pltpu.CompilerParams(collective_id=collective, has_side_effects=True),
    )(x)


def to_columns(x, kernel=True):
    if kernel:
        return lev_exchange(x, 2, 1, 2, 0)
    return lax.all_to_all(x, "lev", 2, 1, tiled=True)


def to_levels(x, kernel=True):
    if kernel:
        return lev_exchange(x, 1, 2, 1, 1)
    return lax.all_to_all(x, "lev", 1, 2, tiled=True)


def level_mix(fields, matrix):
    columns = to_columns(fields)
    mixed = jnp.einsum("abcd,cdij->abij", matrix, columns, precision=lax.Precision.HIGHEST)
    return to_levels(mixed)


def shards(increment, norm_gain, diffusion_i, diffusion_j, sea_mask, coupling):
    steps = 2 * ITERS
    ocean = sea_mask.astype(jnp.float32)
    scaled = ocean[None] * norm_gain * increment
    order_count = coupling.shape[0]
    level_count = order_count // 2
    balance = jnp.eye(order_count, dtype=jnp.float32) + coupling
    forward = balance.reshape(2, level_count, 2, level_count)
    adjoint = jnp.transpose(forward, (2, 3, 0, 1))
    stacked = jnp.stack([diffusion_i, diffusion_j, ocean])
    coefs = (stacked,) + pieces(stacked, 2 * steps, steps)[1:]
    columns = to_columns(scaled, False)
    mixed = jnp.einsum("abcd,cdij->abij", adjoint, columns, precision=lax.Precision.HIGHEST)
    coefs, mixed = lax.optimization_barrier((coefs, mixed))
    adjoint_mixed = to_levels(mixed)
    spread = diffusion(adjoint_mixed, coefs, steps)
    forward_mixed = level_mix(spread, forward)
    return ocean[None] * norm_gain * forward_mixed


def solution(mesh):
    return jax.shard_map(
        shards,
        mesh=mesh,
        in_specs=(
            P(None, "lev", "gx", "gy"),
            P(None, "lev", "gx", "gy"),
            P("lev", "gx", "gy"),
            P("lev", "gx", "gy"),
            P("lev", "gx", "gy"),
            P(),
        ),
        out_specs=P(None, "lev", "gx", "gy"),
        check_vma=False,
    )
```

```python
import functools

import jax
import jax.numpy as jnp
from jax import lax
from jax.experimental import pallas as pl
from jax.experimental.pallas import tpu as pltpu
from jax.sharding import PartitionSpec as P

ITERS = 2
MESH = pl.DeviceIdType.MESH


def pieces(x, height, width):
    fields, levels, rows, cols = x.shape
    up = [(i, (i + 1) % lax.axis_size("gx")) for i in range(lax.axis_size("gx"))]
    down = [(j, i) for i, j in up]
    north = lax.ppermute(x[:, :, rows - height:], "gx", up)
    south = lax.ppermute(x[:, :, :height], "gx", down)
    band = jnp.concatenate([south, north], 2)
    tall = jnp.concatenate([x, band], 2)
    right = [(i, i + 1) for i in range(lax.axis_size("gy") - 1)]
    left = [(j, i) for i, j in right]
    east = lax.ppermute(tall[..., :width], "gy", left)
    west = lax.ppermute(tall[..., cols - width:], "gy", right)
    middle = jnp.zeros((fields, levels, rows + 2 * height, 128 - 2 * width), x.dtype)
    edge = jnp.concatenate([east, middle, west], 3)
    return tall, band, edge


def circular(x, height, width):
    tall, _, edge = pieces(x, height, width)
    return jnp.concatenate([tall, edge], 3)


def plane(t_ref, b_ref, e_ref, f):
    tall = jnp.concatenate([t_ref[f, 0], b_ref[f, 0]], 0)
    return jnp.concatenate([tall, e_ref[f, 0]], 1)


def diffusion_kernel(steps, rows, cols, x_ref, b_ref, e_ref, ct_ref, cb_ref, ce_ref, o_ref):
    height, span = e_ref.shape[2], 2 * e_ref.shape[3]
    fields = o_ref.shape[0]
    along_i = plane(ct_ref, cb_ref, ce_ref, 0)
    along_j = plane(ct_ref, cb_ref, ce_ref, 1)
    sea = plane(ct_ref, cb_ref, ce_ref, 2)
    weight_i = along_i * sea * pltpu.roll(sea, height - 1, 0)
    weight_j = along_j * sea * pltpu.roll(sea, span - 1, 1)
    for f in range(fields):
        values = plane(x_ref, b_ref, e_ref, f)
        for s in range(steps):
            flux_i = weight_i * (pltpu.roll(values, height - 1, 0) - values)
            flux_j = weight_j * (pltpu.roll(values, span - 1, 1) - values)
            values = values + flux_i - pltpu.roll(flux_i, 1, 0) + flux_j - pltpu.roll(flux_j, 1, 1)
        o_ref[f, 0] = values[:rows, :cols]


def diffusion(values, coefs, steps):
    fields, levels, rows, cols = values.shape
    height = rows + 2 * steps
    band = 2 * steps

    def specs(channels):
        return [
            pl.BlockSpec((channels, 1, rows, cols), lambda l: (0, l, 0, 0)),
            pl.BlockSpec((channels, 1, band, cols), lambda l: (0, l, 0, 0)),
            pl.BlockSpec((channels, 1, height, 128), lambda l: (0, l, 0, 0)),
        ]

    _, halo, edge = pieces(values, steps, steps)
    _, coef_halo, coef_edge = coefs
    return pl.pallas_call(
        functools.partial(diffusion_kernel, steps, rows, cols),
        out_shape=jax.ShapeDtypeStruct(values.shape, values.dtype),
        grid=(levels,),
        in_specs=specs(fields) + specs(coef_edge.shape[0]),
        out_specs=pl.BlockSpec((fields, 1, rows, cols), lambda l: (0, l, 0, 0)),
    )(values, halo, edge, coefs[0], coef_halo, coef_edge)


def lev_exchange(x, src_axis, dst_axis, half_axis, collective):
    n = lax.axis_size("lev")
    assert half_axis == src_axis
    out_shape = list(x.shape)
    out_shape[src_axis] //= n
    out_shape[dst_axis] *= n
    src_size = out_shape[src_axis]
    dst_size = x.shape[dst_axis]
    half = src_size // 2
    relay_shape = list(out_shape)
    relay_shape[dst_axis] = dst_size
    relay_shape[half_axis] = half

    def window(axis, start, size, h=None):
        index = [slice(None)] * x.ndim
        index[axis] = pl.ds(start, size)
        if h is not None:
            if half_axis == axis:
                index[axis] = pl.ds(start + h * half, half)
            else:
                index[half_axis] = pl.ds(h * half, half)
        return tuple(index)

    def kernel(x_ref, o_ref, relay, send_sem, recv_sem, local_sem):
        me = lax.axis_index("lev")
        gx = lax.axis_index("gx")
        gy = lax.axis_index("gy")
        right = (me + 1) % n
        left = (me + n - 1) % n
        opposite = (me + 2) % n
        barrier = pltpu.get_barrier_semaphore()
        for peer in (left, right):
            pl.semaphore_signal(barrier, inc=1, device_id=(peer, gx, gy), device_id_type=MESH)
        pl.semaphore_wait(barrier, 2)

        def remote(src, dst, slot, peer):
            return pltpu.make_async_remote_copy(
                src_ref=src, dst_ref=dst, send_sem=send_sem.at[slot], recv_sem=recv_sem.at[slot],
                device_id=(peer, gx, gy), device_id_type=MESH,
            )

        to_right = remote(x_ref.at[window(src_axis, right * src_size, src_size)],
                          o_ref.at[window(dst_axis, me * dst_size, dst_size)], 0, right)
        to_left = remote(x_ref.at[window(src_axis, left * src_size, src_size)],
                         o_ref.at[window(dst_axis, me * dst_size, dst_size)], 1, left)
        via_right = remote(x_ref.at[window(src_axis, opposite * src_size, src_size, 0)], relay.at[0], 2, right)
        via_left = remote(x_ref.at[window(src_axis, opposite * src_size, src_size, 1)], relay.at[1], 3, left)
        for copy in (via_right, via_left, to_right, to_left):
            copy.start()
        local = pltpu.make_async_copy(
            x_ref.at[window(src_axis, me * src_size, src_size)],
            o_ref.at[window(dst_axis, me * dst_size, dst_size)],
            local_sem,
        )
        local.start()
        via_right.wait_recv()
        on_right = remote(relay.at[0], o_ref.at[window(dst_axis, left * dst_size, dst_size, 0)], 4, right)
        on_right.start()
        via_left.wait_recv()
        on_left = remote(relay.at[1], o_ref.at[window(dst_axis, right * dst_size, dst_size, 1)], 5, left)
        on_left.start()
        local.wait()
        via_right.wait_send()
        via_left.wait_send()
        for copy in (to_right, to_left, on_right, on_left):
            copy.wait()

    return pl.pallas_call(
        kernel,
        out_shape=jax.ShapeDtypeStruct(tuple(out_shape), x.dtype),
        in_specs=[pl.BlockSpec(memory_space=pl.ANY)],
        out_specs=pl.BlockSpec(memory_space=pl.ANY),
        scratch_shapes=[
            pltpu.VMEM((2,) + tuple(relay_shape), x.dtype),
            pltpu.SemaphoreType.DMA((6,)),
            pltpu.SemaphoreType.DMA((6,)),
            pltpu.SemaphoreType.DMA,
        ],
        compiler_params=pltpu.CompilerParams(collective_id=collective, has_side_effects=True),
    )(x)


def to_columns(x, kernel=True):
    if kernel:
        return lev_exchange(x, 2, 1, 2, 0)
    return lax.all_to_all(x, "lev", 2, 1, tiled=True)


def to_levels(x, kernel=True):
    if kernel:
        return lev_exchange(x, 1, 2, 1, 1)
    return lax.all_to_all(x, "lev", 1, 2, tiled=True)


def level_mix(fields, matrix):
    columns = to_columns(fields)
    mixed = jnp.einsum("abcd,cdij->abij", matrix, columns, precision=lax.Precision.HIGHEST)
    return to_levels(mixed)


def shards(increment, norm_gain, diffusion_i, diffusion_j, sea_mask, coupling):
    steps = 2 * ITERS
    ocean = sea_mask.astype(jnp.float32)
    scaled = ocean[None] * norm_gain * increment
    order_count = coupling.shape[0]
    level_count = order_count // 2
    balance = jnp.eye(order_count, dtype=jnp.float32) + coupling
    forward = balance.reshape(2, level_count, 2, level_count)
    adjoint = jnp.transpose(forward, (2, 3, 0, 1))
    stacked = jnp.stack([diffusion_i, diffusion_j, ocean])
    coefs = (stacked,) + pieces(stacked, steps, steps)[1:]
    columns = to_columns(scaled, False)
    mixed = jnp.einsum("abcd,cdij->abij", adjoint, columns, precision=lax.Precision.HIGHEST)
    coefs, mixed = lax.optimization_barrier((coefs, mixed))
    adjoint_mixed = to_levels(mixed) * ocean[None]
    spread = diffusion(adjoint_mixed, coefs, steps)
    forward_mixed = level_mix(spread, forward)
    return ocean[None] * norm_gain * forward_mixed


def solution(mesh):
    return jax.shard_map(
        shards,
        mesh=mesh,
        in_specs=(
            P(None, "lev", "gx", "gy"),
            P(None, "lev", "gx", "gy"),
            P("lev", "gx", "gy"),
            P("lev", "gx", "gy"),
            P("lev", "gx", "gy"),
            P(),
        ),
        out_specs=P(None, "lev", "gx", "gy"),
        check_vma=False,
    )
```

```python
import functools

import jax
import jax.numpy as jnp
from jax import lax
from jax.experimental import pallas as pl
from jax.experimental.pallas import tpu as pltpu
from jax.sharding import PartitionSpec as P

ITERS = 2
MESH = pl.DeviceIdType.MESH


def pieces(x, height, width):
    fields, levels, rows, cols = x.shape
    up = [(i, (i + 1) % lax.axis_size("gx")) for i in range(lax.axis_size("gx"))]
    down = [(j, i) for i, j in up]
    north = lax.ppermute(x[:, :, rows - height:], "gx", up)
    south = lax.ppermute(x[:, :, :height], "gx", down)
    tall = jnp.concatenate([x, south, north], 2)
    right = [(i, i + 1) for i in range(lax.axis_size("gy") - 1)]
    left = [(j, i) for i, j in right]
    east = lax.ppermute(tall[..., :width], "gy", left)
    west = lax.ppermute(tall[..., cols - width:], "gy", right)
    return tall, south, north, east, west


def circular(x, height, width):
    tall, _, _, east, west = pieces(x, height, width)
    middle = jnp.zeros(tall.shape[:3] + (128 - 2 * width,), x.dtype)
    return jnp.concatenate([tall, east, middle, west], 3)


def plane(t_ref, s_ref, n_ref, e_ref, w_ref, f):
    tall = jnp.concatenate([t_ref[f, 0], s_ref[f, 0], n_ref[f, 0]], 0)
    east, west = e_ref[f, 0], w_ref[f, 0]
    middle = jnp.zeros((tall.shape[0], 128 - east.shape[1] - west.shape[1]), tall.dtype)
    return jnp.concatenate([tall, east, middle, west], 1)


def diffusion_kernel(steps, rows, cols, x_ref, s_ref, n_ref, e_ref, w_ref, ct_ref, cs_ref, cn_ref, ce_ref, cw_ref, o_ref):
    height, span = e_ref.shape[2], 2 * x_ref.shape[3]
    fields = o_ref.shape[0]
    along_i = plane(ct_ref, cs_ref, cn_ref, ce_ref, cw_ref, 0)
    along_j = plane(ct_ref, cs_ref, cn_ref, ce_ref, cw_ref, 1)
    sea = plane(ct_ref, cs_ref, cn_ref, ce_ref, cw_ref, 2)
    weight_i = along_i * sea * pltpu.roll(sea, height - 1, 0)
    weight_j = along_j * sea * pltpu.roll(sea, span - 1, 1)
    for f in range(fields):
        values = plane(x_ref, s_ref, n_ref, e_ref, w_ref, f)
        for s in range(steps):
            flux_i = weight_i * (pltpu.roll(values, height - 1, 0) - values)
            flux_j = weight_j * (pltpu.roll(values, span - 1, 1) - values)
            values = values + flux_i - pltpu.roll(flux_i, 1, 0) + flux_j - pltpu.roll(flux_j, 1, 1)
        o_ref[f, 0] = values[:rows, :cols]


def diffusion(values, coefs, steps):
    fields, levels, rows, cols = values.shape
    height = rows + 4 * steps
    band = 2 * steps

    def specs(channels):
        return [
            pl.BlockSpec((channels, 1, rows, cols), lambda l: (0, l, 0, 0)),
            pl.BlockSpec((channels, 1, band, cols), lambda l: (0, l, 0, 0)),
            pl.BlockSpec((channels, 1, band, cols), lambda l: (0, l, 0, 0)),
            pl.BlockSpec((channels, 1, height, steps), lambda l: (0, l, 0, 0)),
            pl.BlockSpec((channels, 1, height, steps), lambda l: (0, l, 0, 0)),
        ]

    _, south, north, east, west = pieces(values, band, steps)
    _, coef_south, coef_north, coef_east, coef_west = coefs
    return pl.pallas_call(
        functools.partial(diffusion_kernel, steps, rows, cols),
        out_shape=jax.ShapeDtypeStruct(values.shape, values.dtype),
        grid=(levels,),
        in_specs=specs(fields) + specs(coef_east.shape[0]),
        out_specs=pl.BlockSpec((fields, 1, rows, cols), lambda l: (0, l, 0, 0)),
    )(values, south, north, east, west, coefs[0], coef_south, coef_north, coef_east, coef_west)


def lev_exchange(x, src_axis, dst_axis, half_axis, collective):
    n = lax.axis_size("lev")
    assert half_axis == src_axis
    out_shape = list(x.shape)
    out_shape[src_axis] //= n
    out_shape[dst_axis] *= n
    src_size = out_shape[src_axis]
    dst_size = x.shape[dst_axis]
    half = src_size // 2
    relay_shape = list(out_shape)
    relay_shape[dst_axis] = dst_size
    relay_shape[half_axis] = half

    def window(axis, start, size, h=None):
        index = [slice(None)] * x.ndim
        index[axis] = pl.ds(start, size)
        if h is not None:
            if half_axis == axis:
                index[axis] = pl.ds(start + h * half, half)
            else:
                index[half_axis] = pl.ds(h * half, half)
        return tuple(index)

    def kernel(x_ref, o_ref, relay, send_sem, recv_sem, local_sem):
        me = lax.axis_index("lev")
        gx = lax.axis_index("gx")
        gy = lax.axis_index("gy")
        right = (me + 1) % n
        left = (me + n - 1) % n
        opposite = (me + 2) % n
        barrier = pltpu.get_barrier_semaphore()
        for peer in (left, right):
            pl.semaphore_signal(barrier, inc=1, device_id=(peer, gx, gy), device_id_type=MESH)
        pl.semaphore_wait(barrier, 2)

        def remote(src, dst, slot, peer):
            return pltpu.make_async_remote_copy(
                src_ref=src, dst_ref=dst, send_sem=send_sem.at[slot], recv_sem=recv_sem.at[slot],
                device_id=(peer, gx, gy), device_id_type=MESH,
            )

        to_right = remote(x_ref.at[window(src_axis, right * src_size, src_size)],
                          o_ref.at[window(dst_axis, me * dst_size, dst_size)], 0, right)
        to_left = remote(x_ref.at[window(src_axis, left * src_size, src_size)],
                         o_ref.at[window(dst_axis, me * dst_size, dst_size)], 1, left)
        via_right = remote(x_ref.at[window(src_axis, opposite * src_size, src_size, 0)], relay.at[0], 2, right)
        via_left = remote(x_ref.at[window(src_axis, opposite * src_size, src_size, 1)], relay.at[1], 3, left)
        for copy in (via_right, via_left, to_right, to_left):
            copy.start()
        local = pltpu.make_async_copy(
            x_ref.at[window(src_axis, me * src_size, src_size)],
            o_ref.at[window(dst_axis, me * dst_size, dst_size)],
            local_sem,
        )
        local.start()
        via_right.wait_recv()
        on_right = remote(relay.at[0], o_ref.at[window(dst_axis, left * dst_size, dst_size, 0)], 4, right)
        on_right.start()
        via_left.wait_recv()
        on_left = remote(relay.at[1], o_ref.at[window(dst_axis, right * dst_size, dst_size, 1)], 5, left)
        on_left.start()
        local.wait()
        via_right.wait_send()
        via_left.wait_send()
        for copy in (to_right, to_left, on_right, on_left):
            copy.wait()

    return pl.pallas_call(
        kernel,
        out_shape=jax.ShapeDtypeStruct(tuple(out_shape), x.dtype),
        in_specs=[pl.BlockSpec(memory_space=pl.ANY)],
        out_specs=pl.BlockSpec(memory_space=pl.ANY),
        scratch_shapes=[
            pltpu.VMEM((2,) + tuple(relay_shape), x.dtype),
            pltpu.SemaphoreType.DMA((6,)),
            pltpu.SemaphoreType.DMA((6,)),
            pltpu.SemaphoreType.DMA,
        ],
        compiler_params=pltpu.CompilerParams(collective_id=collective, has_side_effects=True),
    )(x)


def to_columns(x, kernel=True):
    if kernel:
        return lev_exchange(x, 2, 1, 2, 0)
    return lax.all_to_all(x, "lev", 2, 1, tiled=True)


def to_levels(x, kernel=True):
    if kernel:
        return lev_exchange(x, 1, 2, 1, 1)
    return lax.all_to_all(x, "lev", 1, 2, tiled=True)


def level_mix(fields, matrix):
    columns = to_columns(fields)
    mixed = jnp.einsum("abcd,cdij->abij", matrix, columns, precision=lax.Precision.HIGHEST)
    return to_levels(mixed)


def shards(increment, norm_gain, diffusion_i, diffusion_j, sea_mask, coupling):
    steps = 2 * ITERS
    ocean = sea_mask.astype(jnp.float32)
    scaled = ocean[None] * norm_gain * increment
    order_count = coupling.shape[0]
    level_count = order_count // 2
    balance = jnp.eye(order_count, dtype=jnp.float32) + coupling
    forward = balance.reshape(2, level_count, 2, level_count)
    adjoint = jnp.transpose(forward, (2, 3, 0, 1))
    stacked = jnp.stack([diffusion_i, diffusion_j, ocean])
    coefs = (stacked,) + pieces(stacked, 2 * steps, steps)[1:]
    columns = to_columns(scaled, False)
    mixed = jnp.einsum("abcd,cdij->abij", adjoint, columns, precision=lax.Precision.HIGHEST)
    coefs, mixed = lax.optimization_barrier((coefs, mixed))
    adjoint_mixed = to_levels(mixed) * ocean[None]
    spread = diffusion(adjoint_mixed, coefs, steps)
    forward_mixed = level_mix(spread, forward)
    return ocean[None] * norm_gain * forward_mixed


def solution(mesh):
    return jax.shard_map(
        shards,
        mesh=mesh,
        in_specs=(
            P(None, "lev", "gx", "gy"),
            P(None, "lev", "gx", "gy"),
            P("lev", "gx", "gy"),
            P("lev", "gx", "gy"),
            P("lev", "gx", "gy"),
            P(),
        ),
        out_specs=P(None, "lev", "gx", "gy"),
        check_vma=False,
    )
```

```python
import functools

import jax
import jax.numpy as jnp
from jax import lax
from jax.experimental import pallas as pl
from jax.experimental.pallas import tpu as pltpu
from jax.sharding import PartitionSpec as P

ITERS = 2
MESH = pl.DeviceIdType.MESH


def pieces(x, height, width):
    fields, levels, rows, cols = x.shape
    up = [(i, (i + 1) % lax.axis_size("gx")) for i in range(lax.axis_size("gx"))]
    down = [(j, i) for i, j in up]
    north = lax.ppermute(x[:, :, rows - height:], "gx", up)
    south = lax.ppermute(x[:, :, :height], "gx", down)
    tall = jnp.concatenate([x, south, north], 2)
    right = [(i, i + 1) for i in range(lax.axis_size("gy") - 1)]
    left = [(j, i) for i, j in right]
    east = lax.ppermute(tall[..., :width], "gy", left)
    west = lax.ppermute(tall[..., cols - width:], "gy", right)
    middle = jnp.zeros((fields, levels, rows + 2 * height, 128 - 2 * width), x.dtype)
    edge = jnp.concatenate([east, middle, west], 3)
    return tall, south, north, edge


def circular(x, height, width):
    tall, _, _, edge = pieces(x, height, width)
    return jnp.concatenate([tall, edge], 3)


def plane(t_ref, s_ref, n_ref, e_ref, f):
    tall = jnp.concatenate([t_ref[f, 0], s_ref[f, 0], n_ref[f, 0]], 0)
    return jnp.concatenate([tall, e_ref[f, 0]], 1)


def diffusion_kernel(steps, rows, cols, x_ref, s_ref, n_ref, e_ref, ct_ref, cs_ref, cn_ref, ce_ref, o_ref):
    height, span = e_ref.shape[2], 2 * e_ref.shape[3]
    fields = o_ref.shape[0]
    along_i = plane(ct_ref, cs_ref, cn_ref, ce_ref, 0)
    along_j = plane(ct_ref, cs_ref, cn_ref, ce_ref, 1)
    sea = (along_i > 0).astype(along_i.dtype)
    weight_i = along_i * pltpu.roll(sea, height - 1, 0)
    weight_j = along_j * pltpu.roll(sea, span - 1, 1)
    for f in range(fields):
        values = plane(x_ref, s_ref, n_ref, e_ref, f)
        for s in range(steps):
            flux_i = weight_i * (pltpu.roll(values, height - 1, 0) - values)
            flux_j = weight_j * (pltpu.roll(values, span - 1, 1) - values)
            values = values + flux_i - pltpu.roll(flux_i, 1, 0) + flux_j - pltpu.roll(flux_j, 1, 1)
        o_ref[f, 0] = values[:rows, :cols]


def diffusion(values, coefs, steps):
    fields, levels, rows, cols = values.shape
    height = rows + 4 * steps
    band = 2 * steps

    def specs(channels):
        return [
            pl.BlockSpec((channels, 1, rows, cols), lambda l: (0, l, 0, 0)),
            pl.BlockSpec((channels, 1, band, cols), lambda l: (0, l, 0, 0)),
            pl.BlockSpec((channels, 1, band, cols), lambda l: (0, l, 0, 0)),
            pl.BlockSpec((channels, 1, height, 128), lambda l: (0, l, 0, 0)),
        ]

    _, south, north, edge = pieces(values, band, steps)
    _, coef_south, coef_north, coef_edge = coefs
    return pl.pallas_call(
        functools.partial(diffusion_kernel, steps, rows, cols),
        out_shape=jax.ShapeDtypeStruct(values.shape, values.dtype),
        grid=(levels,),
        in_specs=specs(fields) + specs(coef_edge.shape[0]),
        out_specs=pl.BlockSpec((fields, 1, rows, cols), lambda l: (0, l, 0, 0)),
    )(values, south, north, edge, coefs[0], coef_south, coef_north, coef_edge)


def lev_exchange(x, src_axis, dst_axis, half_axis, collective):
    n = lax.axis_size("lev")
    assert half_axis == src_axis
    out_shape = list(x.shape)
    out_shape[src_axis] //= n
    out_shape[dst_axis] *= n
    src_size = out_shape[src_axis]
    dst_size = x.shape[dst_axis]
    half = src_size // 2
    relay_shape = list(out_shape)
    relay_shape[dst_axis] = dst_size
    relay_shape[half_axis] = half

    def window(axis, start, size, h=None):
        index = [slice(None)] * x.ndim
        index[axis] = pl.ds(start, size)
        if h is not None:
            if half_axis == axis:
                index[axis] = pl.ds(start + h * half, half)
            else:
                index[half_axis] = pl.ds(h * half, half)
        return tuple(index)

    def kernel(x_ref, o_ref, relay, send_sem, recv_sem, local_sem):
        me = lax.axis_index("lev")
        gx = lax.axis_index("gx")
        gy = lax.axis_index("gy")
        right = (me + 1) % n
        left = (me + n - 1) % n
        opposite = (me + 2) % n
        barrier = pltpu.get_barrier_semaphore()
        for peer in (left, right):
            pl.semaphore_signal(barrier, inc=1, device_id=(peer, gx, gy), device_id_type=MESH)
        pl.semaphore_wait(barrier, 2)

        def remote(src, dst, slot, peer):
            return pltpu.make_async_remote_copy(
                src_ref=src, dst_ref=dst, send_sem=send_sem.at[slot], recv_sem=recv_sem.at[slot],
                device_id=(peer, gx, gy), device_id_type=MESH,
            )

        to_right = remote(x_ref.at[window(src_axis, right * src_size, src_size)],
                          o_ref.at[window(dst_axis, me * dst_size, dst_size)], 0, right)
        to_left = remote(x_ref.at[window(src_axis, left * src_size, src_size)],
                         o_ref.at[window(dst_axis, me * dst_size, dst_size)], 1, left)
        via_right = remote(x_ref.at[window(src_axis, opposite * src_size, src_size, 0)], relay.at[0], 2, right)
        via_left = remote(x_ref.at[window(src_axis, opposite * src_size, src_size, 1)], relay.at[1], 3, left)
        for copy in (via_right, via_left, to_right, to_left):
            copy.start()
        local = pltpu.make_async_copy(
            x_ref.at[window(src_axis, me * src_size, src_size)],
            o_ref.at[window(dst_axis, me * dst_size, dst_size)],
            local_sem,
        )
        local.start()
        via_right.wait_recv()
        on_right = remote(relay.at[0], o_ref.at[window(dst_axis, left * dst_size, dst_size, 0)], 4, right)
        on_right.start()
        via_left.wait_recv()
        on_left = remote(relay.at[1], o_ref.at[window(dst_axis, right * dst_size, dst_size, 1)], 5, left)
        on_left.start()
        local.wait()
        via_right.wait_send()
        via_left.wait_send()
        for copy in (to_right, to_left, on_right, on_left):
            copy.wait()

    return pl.pallas_call(
        kernel,
        out_shape=jax.ShapeDtypeStruct(tuple(out_shape), x.dtype),
        in_specs=[pl.BlockSpec(memory_space=pl.ANY)],
        out_specs=pl.BlockSpec(memory_space=pl.ANY),
        scratch_shapes=[
            pltpu.VMEM((2,) + tuple(relay_shape), x.dtype),
            pltpu.SemaphoreType.DMA((6,)),
            pltpu.SemaphoreType.DMA((6,)),
            pltpu.SemaphoreType.DMA,
        ],
        compiler_params=pltpu.CompilerParams(collective_id=collective, has_side_effects=True),
    )(x)


def to_columns(x, kernel=True):
    if kernel:
        return lev_exchange(x, 2, 1, 2, 0)
    return lax.all_to_all(x, "lev", 2, 1, tiled=True)


def to_levels(x, kernel=True):
    if kernel:
        return lev_exchange(x, 1, 2, 1, 1)
    return lax.all_to_all(x, "lev", 1, 2, tiled=True)


def level_mix(fields, matrix):
    columns = to_columns(fields)
    mixed = jnp.einsum("abcd,cdij->abij", matrix, columns, precision=lax.Precision.HIGHEST)
    return to_levels(mixed)


def shards(increment, norm_gain, diffusion_i, diffusion_j, sea_mask, coupling):
    steps = 2 * ITERS
    ocean = sea_mask.astype(jnp.float32)
    scaled = ocean[None] * norm_gain * increment
    order_count = coupling.shape[0]
    level_count = order_count // 2
    balance = jnp.eye(order_count, dtype=jnp.float32) + coupling
    forward = balance.reshape(2, level_count, 2, level_count)
    adjoint = jnp.transpose(forward, (2, 3, 0, 1))
    stacked = jnp.stack([diffusion_i * ocean, diffusion_j * ocean])
    coefs = (stacked,) + pieces(stacked, 2 * steps, steps)[1:]
    columns = to_columns(scaled, False)
    mixed = jnp.einsum("abcd,cdij->abij", adjoint, columns, precision=lax.Precision.HIGHEST)
    coefs, mixed = lax.optimization_barrier((coefs, mixed))
    adjoint_mixed = to_levels(mixed) * ocean[None]
    spread = diffusion(adjoint_mixed, coefs, steps)
    forward_mixed = level_mix(spread, forward)
    return ocean[None] * norm_gain * forward_mixed


def solution(mesh):
    return jax.shard_map(
        shards,
        mesh=mesh,
        in_specs=(
            P(None, "lev", "gx", "gy"),
            P(None, "lev", "gx", "gy"),
            P("lev", "gx", "gy"),
            P("lev", "gx", "gy"),
            P("lev", "gx", "gy"),
            P(),
        ),
        out_specs=P(None, "lev", "gx", "gy"),
        check_vma=False,
    )
```

```python
import functools

import jax
import jax.numpy as jnp
from jax import lax
from jax.experimental import pallas as pl
from jax.experimental.pallas import tpu as pltpu
from jax.sharding import PartitionSpec as P

ITERS = 2
MESH = pl.DeviceIdType.MESH


def pieces(x, height, width):
    fields, levels, rows, cols = x.shape
    up = [(i, (i + 1) % lax.axis_size("gx")) for i in range(lax.axis_size("gx"))]
    down = [(j, i) for i, j in up]
    north = lax.ppermute(x[:, :, rows - height:], "gx", up)
    south = lax.ppermute(x[:, :, :height], "gx", down)
    tall = jnp.concatenate([x, south, north], 2)
    right = [(i, i + 1) for i in range(lax.axis_size("gy") - 1)]
    left = [(j, i) for i, j in right]
    east = lax.ppermute(tall[..., :width], "gy", left)
    west = lax.ppermute(tall[..., cols - width:], "gy", right)
    middle = jnp.zeros((fields, levels, rows + 2 * height, 128 - 2 * width), x.dtype)
    edge = jnp.concatenate([east, middle, west], 3)
    return tall, south, north, edge


def circular(x, height, width):
    tall, _, _, edge = pieces(x, height, width)
    return jnp.concatenate([tall, edge], 3)


def plane(center, s_ref, n_ref, e_ref, f):
    tall = jnp.concatenate([center, s_ref[f, 0], n_ref[f, 0]], 0)
    return jnp.concatenate([tall, e_ref[f, 0]], 1)


def diffusion_kernel(steps, rows, cols, x_ref, ct_ref, s_ref, n_ref, e_ref, o_ref):
    height, span = e_ref.shape[2], 2 * e_ref.shape[3]
    fields = o_ref.shape[0]
    along_i = plane(ct_ref[0, 0], s_ref, n_ref, e_ref, fields)
    along_j = plane(ct_ref[1, 0], s_ref, n_ref, e_ref, fields + 1)
    sea = (along_i > 0).astype(along_i.dtype)
    weight_i = along_i * pltpu.roll(sea, height - 1, 0)
    weight_j = along_j * pltpu.roll(sea, span - 1, 1)
    for f in range(fields):
        values = plane(x_ref[f, 0], s_ref, n_ref, e_ref, f)
        for s in range(steps):
            flux_i = weight_i * (pltpu.roll(values, height - 1, 0) - values)
            flux_j = weight_j * (pltpu.roll(values, span - 1, 1) - values)
            values = values + flux_i - pltpu.roll(flux_i, 1, 0) + flux_j - pltpu.roll(flux_j, 1, 1)
        o_ref[f, 0] = values[:rows, :cols]


def diffusion(values, coefs, steps):
    fields, levels, rows, cols = values.shape
    height = rows + 4 * steps
    band = 2 * steps
    channels = fields + coefs.shape[0]
    _, south, north, edge = pieces(jnp.concatenate([values, coefs]), band, steps)
    return pl.pallas_call(
        functools.partial(diffusion_kernel, steps, rows, cols),
        out_shape=jax.ShapeDtypeStruct(values.shape, values.dtype),
        grid=(levels,),
        in_specs=[
            pl.BlockSpec((fields, 1, rows, cols), lambda l: (0, l, 0, 0)),
            pl.BlockSpec((coefs.shape[0], 1, rows, cols), lambda l: (0, l, 0, 0)),
            pl.BlockSpec((channels, 1, band, cols), lambda l: (0, l, 0, 0)),
            pl.BlockSpec((channels, 1, band, cols), lambda l: (0, l, 0, 0)),
            pl.BlockSpec((channels, 1, height, 128), lambda l: (0, l, 0, 0)),
        ],
        out_specs=pl.BlockSpec((fields, 1, rows, cols), lambda l: (0, l, 0, 0)),
    )(values, coefs, south, north, edge)


def lev_exchange(x, src_axis, dst_axis, half_axis, collective):
    n = lax.axis_size("lev")
    assert half_axis == src_axis
    out_shape = list(x.shape)
    out_shape[src_axis] //= n
    out_shape[dst_axis] *= n
    src_size = out_shape[src_axis]
    dst_size = x.shape[dst_axis]
    half = src_size // 2
    relay_shape = list(out_shape)
    relay_shape[dst_axis] = dst_size
    relay_shape[half_axis] = half

    def window(axis, start, size, h=None):
        index = [slice(None)] * x.ndim
        index[axis] = pl.ds(start, size)
        if h is not None:
            if half_axis == axis:
                index[axis] = pl.ds(start + h * half, half)
            else:
                index[half_axis] = pl.ds(h * half, half)
        return tuple(index)

    def kernel(x_ref, o_ref, relay, send_sem, recv_sem, local_sem):
        me = lax.axis_index("lev")
        gx = lax.axis_index("gx")
        gy = lax.axis_index("gy")
        right = (me + 1) % n
        left = (me + n - 1) % n
        opposite = (me + 2) % n
        barrier = pltpu.get_barrier_semaphore()
        for peer in (left, right):
            pl.semaphore_signal(barrier, inc=1, device_id=(peer, gx, gy), device_id_type=MESH)
        pl.semaphore_wait(barrier, 2)

        def remote(src, dst, slot, peer):
            return pltpu.make_async_remote_copy(
                src_ref=src, dst_ref=dst, send_sem=send_sem.at[slot], recv_sem=recv_sem.at[slot],
                device_id=(peer, gx, gy), device_id_type=MESH,
            )

        to_right = remote(x_ref.at[window(src_axis, right * src_size, src_size)],
                          o_ref.at[window(dst_axis, me * dst_size, dst_size)], 0, right)
        to_left = remote(x_ref.at[window(src_axis, left * src_size, src_size)],
                         o_ref.at[window(dst_axis, me * dst_size, dst_size)], 1, left)
        via_right = remote(x_ref.at[window(src_axis, opposite * src_size, src_size, 0)], relay.at[0], 2, right)
        via_left = remote(x_ref.at[window(src_axis, opposite * src_size, src_size, 1)], relay.at[1], 3, left)
        for copy in (via_right, via_left, to_right, to_left):
            copy.start()
        local = pltpu.make_async_copy(
            x_ref.at[window(src_axis, me * src_size, src_size)],
            o_ref.at[window(dst_axis, me * dst_size, dst_size)],
            local_sem,
        )
        local.start()
        via_right.wait_recv()
        on_right = remote(relay.at[0], o_ref.at[window(dst_axis, left * dst_size, dst_size, 0)], 4, right)
        on_right.start()
        via_left.wait_recv()
        on_left = remote(relay.at[1], o_ref.at[window(dst_axis, right * dst_size, dst_size, 1)], 5, left)
        on_left.start()
        local.wait()
        via_right.wait_send()
        via_left.wait_send()
        for copy in (to_right, to_left, on_right, on_left):
            copy.wait()

    return pl.pallas_call(
        kernel,
        out_shape=jax.ShapeDtypeStruct(tuple(out_shape), x.dtype),
        in_specs=[pl.BlockSpec(memory_space=pl.ANY)],
        out_specs=pl.BlockSpec(memory_space=pl.ANY),
        scratch_shapes=[
            pltpu.VMEM((2,) + tuple(relay_shape), x.dtype),
            pltpu.SemaphoreType.DMA((6,)),
            pltpu.SemaphoreType.DMA((6,)),
            pltpu.SemaphoreType.DMA,
        ],
        compiler_params=pltpu.CompilerParams(collective_id=collective, has_side_effects=True),
    )(x)


def to_columns(x, kernel=True):
    if kernel:
        return lev_exchange(x, 2, 1, 2, 0)
    return lax.all_to_all(x, "lev", 2, 1, tiled=True)


def to_levels(x, kernel=True):
    if kernel:
        return lev_exchange(x, 1, 2, 1, 1)
    return lax.all_to_all(x, "lev", 1, 2, tiled=True)


def level_mix(fields, matrix):
    columns = to_columns(fields)
    mixed = jnp.einsum("abcd,cdij->abij", matrix, columns, precision=lax.Precision.HIGHEST)
    return to_levels(mixed)


def shards(increment, norm_gain, diffusion_i, diffusion_j, sea_mask, coupling):
    steps = 2 * ITERS
    ocean = sea_mask.astype(jnp.float32)
    scaled = ocean[None] * norm_gain * increment
    order_count = coupling.shape[0]
    level_count = order_count // 2
    balance = jnp.eye(order_count, dtype=jnp.float32) + coupling
    forward = balance.reshape(2, level_count, 2, level_count)
    adjoint = jnp.transpose(forward, (2, 3, 0, 1))
    coefs = jnp.stack([diffusion_i * ocean, diffusion_j * ocean])
    adjoint_mixed = level_mix(scaled, adjoint) * ocean[None]
    spread = diffusion(adjoint_mixed, coefs, steps)
    forward_mixed = level_mix(spread, forward)
    return ocean[None] * norm_gain * forward_mixed


def solution(mesh):
    return jax.shard_map(
        shards,
        mesh=mesh,
        in_specs=(
            P(None, "lev", "gx", "gy"),
            P(None, "lev", "gx", "gy"),
            P("lev", "gx", "gy"),
            P("lev", "gx", "gy"),
            P("lev", "gx", "gy"),
            P(),
        ),
        out_specs=P(None, "lev", "gx", "gy"),
        check_vma=False,
    )
```
